128 devices in a mesh: tile: 32 (over y, z, core), grp: 4 (over x).
Axes of the slice: x: 4, y: 4, z: 4, core: 2. Of those that a mesh axis runs over, the one named last changes fastest.
Arguments:
- soil_water: float32 [6, 8388608], P(None, ('tile', 'grp')), may hold values from 0.1 to 0.9
- rainfall: float32 [8388608], P(('tile', 'grp')), may hold values from 0.005 to 0.2
- drain_coef: float32 [6, 8388608], P(None, ('tile', 'grp')), may hold values from 0.02 to 0.5
- cell_storage: float32 [8388608], P(('tile', 'grp')), may hold values from 0.01 to 2
- release_rate: float32 [8388608], P(('tile', 'grp')), may hold values from 0.05 to 0.8
- downstream: int32 [8388608], P(('tile', 'grp')), may hold values from 1 to 128, as said below
- block_owner: int32 [65536, 1], P(('tile', 'grp')), may hold values from 0 to 127; in each aligned block of 512 rows (0 to 511, 512 to 1023, ...) at most 8 rows name the same one
- outlet_reach: int32 [65536], P(('tile', 'grp')), may hold values from 0 to 127
- river_storage: float32 [4, 4096], P('grp', 'tile'), may hold values from 0.02 to 0.5
- river_lag: float32 [4, 4096], P('grp', 'tile'), may hold values from 0 to 1
Outputs:
- soil_out: float32 [6, 8388608], P(None, ('tile', 'grp'))
- storage_out: float32 [8388608], P(('tile', 'grp'))
- section: float32 [4, 4096], P('grp', 'tile')
The draws below stay inside these ranges and needn't reach their ends.
Inputs may be any that keep to these rules, and one draw needn't show every extreme that they name: `downstream`: within its block of 128 cells a cell drains to a later cell of the block, or to 128, the block's outlet. `block_owner`: of the 512 blocks of one device, at most 8 have the same owner.
All inputs are finite; a program needn't handle non-finite values.
Results may differ from the reference program's by a relative error of at most 0.0003.
Values sent between devices are 32-bit elements; how exact they have to be, the bound alone decides.
No kernel may reach another device: no remote copies, remote signals or barrier semaphores. Data moves between devices by JAX's collectives and lax.ppermute only.
A program may use at most 64 MiB of HBM per device.

```python
import math
import jax
import jax.numpy as jnp
import numpy as np
from jax import lax

SOIL = 6
CELL = 128
BLK_DEV = 512
REACH = 128
SUB = 4
CAP = 8
RIVERS = 4
RIVER_LEN = 4096
NBLOCKS = 65536
LAND = 8388608
DEVICES = 128


def draw_downstream(key, part):
    position = jnp.arange(LAND, dtype=jnp.int32) % CELL
    return jax.random.randint(key, (LAND,), position + 1, CELL + 1).astype(jnp.int32)


def draw_river_lag(key, part):
    stochastic_root_token, stochastic_placement_token, stochastic_downpour_token = jax.random.split(jax.random.fold_in(key, 7), 3)
    tensor_extents = (RIVERS, RIVER_LEN)
    spread = jnp.exp(jax.random.uniform(stochastic_root_token, tensor_extents, jnp.float32, jnp.log(0.2), jnp.log(2.0)))
    starting_integer_entropy = spread / RIVER_LEN
    spots = jax.random.randint(stochastic_placement_token, (RIVERS, 3), 0, RIVER_LEN)
    places = jnp.arange(RIVER_LEN, dtype=jnp.int32)
    deluged_grid_points = jnp.any(places[None, :, None] == spots[:, None, :], axis=2)
    sudden_downpour_episode = jax.random.uniform(stochastic_downpour_token, tensor_extents, jnp.float32, 0.25, 1.0)
    return jnp.where(deluged_grid_points, sudden_downpour_episode, starting_integer_entropy).astype(jnp.float32)


def set_ends(array, own_key, smallest, largest):
    place = [jax.random.randint(jax.random.fold_in(own_key, axis), (), 0, length) for axis, length in enumerate(array.shape)]
    widest = array.shape.index(max(array.shape))
    beside = place[:widest] + [(place[widest] + 1) % array.shape[widest]] + place[widest + 1:]
    return array.at[tuple(place)].set(smallest).at[tuple(beside)].set(largest)


def block_levels(rng, extent, cuts, least, high):
    def one(dim, shards_of):
        steps = jax.random.uniform(jax.random.fold_in(jax.random.fold_in(rng, 6), dim), (shards_of,), jnp.float32, least / len(cuts), high / len(cuts))
        return jnp.repeat(jnp.exp(steps), extent[dim] // shards_of).reshape((-1,) + (1,) * (len(extent) - dim - 1))

    level = one(*cuts[0])
    for cut in cuts[1:]:
        level = level * one(*cut)
    return level


def shared_out(stream_key, own, number, rows, number_of, top, reach, lean):
    order = jax.random.permutation(stream_key, number_of)
    crowded, usual = portions_of(number_of, rows * top, reach, lean, True), portions_of(number_of, rows * top, reach, lean, False)
    places = jnp.arange(number_of)

    def named(lengths, turn):
        used = int((lengths > 0).sum())
        fixed = max(1, used // 4)
        shifted = fixed + (places - fixed + turn * (used - fixed)) % max(1, number_of - fixed)
        return jnp.zeros((number_of,), jnp.int32).at[order[jnp.where(places < fixed, places, shifted)]].set(jnp.asarray(lengths, jnp.int32))

    lengths = jnp.where(number % 4 == 0, named(crowded, number // 4), named(usual, number - number // 4 - 1))
    mixed = jax.random.permutation(jax.random.fold_in(own, 3), number_of)
    donor, receiver = mixed[0:number_of // 2 * 2:2], mixed[1:number_of // 2 * 2:2]
    slack = jnp.minimum(lengths[donor] - 1, reach - lengths[receiver]) // 2
    slack = jnp.where((donor == order[0]) | (receiver == order[0]) | (lengths[receiver] == 0), 0, jnp.maximum(slack, 0))
    shifted = jax.random.randint(jax.random.fold_in(own, 4), (number_of // 2,), 0, 1 << 20) % (slack + 1)
    lengths = lengths.at[donor].add(-shifted).at[receiver].add(shifted)
    items = jnp.searchsorted(jnp.cumsum(lengths), jnp.arange(rows * top), side="right").astype(jnp.int32)
    grid = items.reshape(top, rows).T
    grid = grid[jax.random.permutation(jax.random.fold_in(own, 1), rows)]
    turn = jax.random.randint(jax.random.fold_in(own, 2), (rows, 1), 0, top)
    return jnp.take_along_axis(grid, (jnp.arange(top)[None, :] + turn) % top, axis=1)


def portions_of(count, total, reach, lean, full):
    loads = [(1 << 20) // math.isqrt(rank ** lean) + 1 for rank in range(1, count + 1)]
    largest = reach if full else min(reach, max(-(-total // count), total * loads[0] // sum(loads)))
    least = 1 if total - largest >= count - 1 else 0
    holding, spare = [largest] + [least] * (count - 1), total - largest - least * (count - 1)
    while spare > 0:
        free = [i for i in range(1, count) if holding[i] < largest] or [i for i in range(1, count) if holding[i] < reach]
        mass, remaining = sum([loads[i] for i in free]), spare
        for i in free:
            more = min(reach - holding[i], max(1, remaining * loads[i] // mass), spare)
            holding[i] = holding[i] + more
            spare = spare - more
    return np.array(holding)


def setup_inputs(seed: int = 0) -> dict:
    keys = jax.random.split(jax.random.key(seed), 11)
    soil_water = jnp.clip(0.1 + 0.79999997 * jax.random.uniform(keys[0], (SOIL, LAND), jnp.float32) ** block_levels(keys[0], (SOIL, LAND), ((1, 128),), -0.2, 0.2), 0.1, 0.9)
    rainfall = jnp.clip(jnp.exp(math.log(0.2) - 3.6888795 * jax.random.uniform(keys[1], (LAND,), jnp.float32) ** block_levels(keys[1], (LAND,), ((0, 128),), -0.2, 0.2)), 0.005, 0.2)
    drain_coef = jnp.clip(jnp.exp(math.log(0.5) - 3.218876 * jax.random.uniform(keys[2], (SOIL, LAND), jnp.float32) ** block_levels(keys[2], (SOIL, LAND), ((1, 128),), -0.2, 0.2)), 0.02, 0.5)
    cell_storage = jnp.clip(jnp.exp(math.log(2.0) - 5.2983174 * jax.random.uniform(keys[3], (LAND,), jnp.float32) ** block_levels(keys[3], (LAND,), ((0, 128),), -0.2, 0.2)), 0.01, 2.0)
    release_rate = jnp.clip(jnp.exp(math.log(0.8) - 2.7725887 * jax.random.uniform(keys[4], (LAND,), jnp.float32) ** block_levels(keys[4], (LAND,), ((0, 128),), -0.2, 0.2)), 0.05, 0.8)
    downstream = draw_downstream(jax.random.fold_in(keys[10], 71), 0)
    block_owner_keys = jax.random.split(jax.random.fold_in(keys[6], 1), NBLOCKS // BLK_DEV)
    block_owner_turns = jax.random.permutation(jax.random.fold_in(keys[6], 3), NBLOCKS // BLK_DEV)
    block_owner = jax.vmap(lambda own, number: shared_out(jax.random.fold_in(keys[6], 2), own, number, BLK_DEV, DEVICES, 1, CAP, 2))(block_owner_keys, block_owner_turns).reshape((NBLOCKS, 1))
    outlet_reach = set_ends(jax.random.randint(keys[7], (NBLOCKS,), 0, REACH), jax.random.fold_in(keys[7], 1), 0, REACH - 1).astype(jnp.int32)
    river_storage = jnp.clip(jnp.exp(math.log(0.5) - 3.218876 * jax.random.uniform(keys[8], (RIVERS, RIVER_LEN), jnp.float32) ** block_levels(keys[8], (RIVERS, RIVER_LEN), ((0, 4), (1, 32)), -0.2, 0.2)), 0.02, 0.5)
    river_lag = draw_river_lag(jax.random.fold_in(keys[10], 71), 0)
    return {"soil_water": soil_water, "rainfall": rainfall, "drain_coef": drain_coef, "cell_storage": cell_storage, "release_rate": release_rate, "downstream": downstream, "block_owner": block_owner, "outlet_reach": outlet_reach, "river_storage": river_storage, "river_lag": river_lag}


recharge_share = 0.2


def land_step(soil_water, rainfall, drain_coef):
    top_layer = soil_water[0]
    surface = rainfall * top_layer * top_layer
    soaked = rainfall - surface
    drained = drain_coef * soil_water * soil_water * soil_water
    inflow = jnp.concatenate([soaked[None], drained[:-1]], axis=0)
    return soil_water + inflow - drained, surface + drained[-1]


def route_turn(storage, share, release_rate, downstream, back):
    width = storage.shape[-1]
    targets = jnp.arange(width, dtype=jnp.int32)
    links = (downstream[:, :, None] == targets[None, None, :]).astype(jnp.float32)
    leaving = (downstream == width).astype(jnp.float32)
    factor = jnp.where(downstream == width, back[:, None], 1.0)
    release = release_rate * storage * factor
    upstream = jnp.einsum("gk,gki->gi", release, links, precision=lax.Precision.HIGHEST)
    outlet = jnp.sum(release * leaving, axis=1)
    return storage + share + upstream - release, outlet


def reference(soil_water, rainfall, drain_coef, cell_storage, release_rate, downstream, block_owner, outlet_reach, river_storage, river_lag):
    soil_mid, runoff = land_step(soil_water, rainfall, drain_coef)

    def blocked(values):
        return values.reshape(DEVICES, BLK_DEV, CELL)

    share = blocked(runoff / SUB)
    rates = blocked(release_rate)
    links = blocked(downstream)
    storage = blocked(cell_storage)
    owner = block_owner[:, 0].astype(jnp.int32)
    river_index = owner % RIVERS
    segment = owner // RIVERS
    position = (river_index * RIVER_LEN + segment * REACH + outlet_reach).astype(jnp.int32)
    weight = 1.0 / (1.0 + river_lag)
    volume = river_storage

    def advance(previous, column):
        flow_now = column[0] * previous + column[1]
        return flow_now, flow_now

    def route_device(parts):
        return route_turn(parts[0], parts[1], parts[2], parts[3], parts[4])

    flow = volume
    for turn in range(SUB):
        back = (1.0 / (1.0 + volume.reshape(-1)[position])).reshape(DEVICES, BLK_DEV)
        storage, outlets = lax.map(route_device, (storage, share, rates, links, back))
        lateral = jax.ops.segment_sum(outlets.reshape(-1), position, num_segments=RIVERS * RIVER_LEN) / CELL
        feed = weight * (volume + lateral.reshape(RIVERS, RIVER_LEN))
        _, flows = lax.scan(advance, jnp.zeros((RIVERS,), jnp.float32), (weight.T, feed.T))
        flow = flows.T
        volume = river_lag * flow
    section = jnp.log1p(flow)
    storage_out = storage.reshape(-1)
    flooded = storage_out / (storage_out + 1.0)
    soil_out = soil_mid.at[0].add(recharge_share * flooded * (1.0 - soil_mid[0]))
    return soil_out, storage_out, section
```

```python
import jax
import jax.numpy as jnp
from jax import lax
from jax.experimental import pallas as pl
from jax.experimental.pallas import tpu as pltpu
from jax.sharding import PartitionSpec as P

SUB = 4
recharge_share = 0.2

W = 128
CHUNK = 128
FIELDS = 9
MB = 1024 * 1024


def gat(values, index):
    return jnp.take_along_axis(values, index, axis=1, mode="promise_in_bounds")


def iota(shape, dim):
    return lax.broadcasted_iota(jnp.int32, shape, dim)


def split3(x):
    hi = x.astype(jnp.bfloat16)
    rest = x - hi.astype(jnp.float32)
    mid = rest.astype(jnp.bfloat16)
    low = (rest - mid.astype(jnp.float32)).astype(jnp.bfloat16)
    return hi, mid, low


def pick(onehot, x):
    hi, mid, low = split3(x)
    dot = lambda part: jnp.dot(onehot, part, preferred_element_type=jnp.float32)
    return dot(hi) + dot(mid) + dot(low)


def moments_kernel(
    soil, coef, rain, storage, rate, links, owner, reach, send, packed, carry
):
    step = pl.program_id(0)
    lane = iota((CHUNK, W), 1)
    sub = iota((CHUNK, W), 0)
    own = jnp.broadcast_to(owner[pl.ds(step, 1), :], (W, CHUNK))
    hit = (own == sub).astype(jnp.float32)
    hit16 = hit.astype(jnp.bfloat16)

    @pl.when(step == 0)
    def _():
        send[...] = jnp.zeros_like(send)
        carry[...] = jnp.zeros_like(carry)

    before = (sub < lane).astype(jnp.bfloat16)
    seen = jnp.dot(hit16, before, preferred_element_type=jnp.float32) + carry[...]
    carry[...] += jnp.sum(hit, axis=1, keepdims=True)
    rank = jnp.sum(hit * seen, axis=0, keepdims=True)
    both = rank + 8.0 * reach[pl.ds(step, 1), :].astype(jnp.float32)
    both = jnp.transpose(jnp.broadcast_to(both, (W, CHUNK))).astype(jnp.int32)
    packed[...] = both.astype(jnp.float32)

    rows = 32

    def body(i, _):
        at = pl.ds(pl.multiple_of(i * rows, rows), rows)
        w0, w5, c5 = soil[at, 0, :], soil[at, 5, :], coef[at, 5, :]
        s, r, down = storage[at, :], rate[at, :], links[at, :]
        share = (rain[at, :] * w0 * w0 + c5 * w5 * w5 * w5) * (1.0 / SUB)
        leaves = down == W
        to = down & (W - 1)
        follow = lambda v: jnp.where(leaves, 0.0, gat(v, to))
        a1 = jnp.where(leaves, r, 0.0)
        a2 = a1 * r
        a3 = a2 * r
        g = follow(a1)
        w_1 = r * g
        w_2 = w_1 * g
        w_3 = w_2 * g
        x_1 = r * follow(w_1)
        x_2 = r * follow(w_2)
        z = w_1 * (1.0 - r) + x_1
        y = r * follow(z)
        e1 = (1.0 - r) * s + share
        h1 = a1 * share
        h2 = a2 * share
        terms = (
            a1 * s,
            a2 * s,
            a3 * s,
            a3 * r * s,
            h1 + w_1 * s,
            h2 + w_2 * s,
            a3 * share + w_3 * s,
            h1 + w_1 * e1 + x_1 * s,
            h2 + w_2 * e1 + x_2 * s,
            h1 + w_1 * share + z * e1 + y * s,
        )
        lane = iota((rows, W), 1)
        field = lane & 15
        both = packed[at, :].astype(jnp.int32)
        out = (both >> 3).astype(jnp.float32)
        for f, term in enumerate(terms):
            out = jnp.where(field == f, jnp.sum(term, axis=1, keepdims=True), out)
        packed[at, :] = jnp.where((lane >> 4) == (both & 7), out, 0.0)
        return 0

    lax.fori_loop(0, CHUNK // rows, body, 0)
    send[...] += pick(hit16, packed[...])


def inflow_kernel(soil, coef, rain, storage, rate, links, owner, reach, soil_mid, gains, hit, spot):
    step = pl.program_id(0)
    rows = 32
    sub = iota((CHUNK, W), 0)
    own = jnp.broadcast_to(owner[pl.ds(step, 1), :], (W, CHUNK))
    hit[...] = jnp.transpose((own == sub).astype(jnp.float32)).astype(jnp.bfloat16)
    at_reach = jnp.broadcast_to(reach[pl.ds(step, 1), :].astype(jnp.float32), (W, CHUNK))
    spot[...] = jnp.transpose(at_reach).astype(jnp.int32)

    def body(i, _):
        at = pl.ds(pl.multiple_of(i * rows, rows), rows)
        lane = iota((rows, W), 1)
        rainfall = rain[at, :]
        w0 = soil[at, 0, :]
        surface = rainfall * w0 * w0
        coming = rainfall - surface
        for layer in range(6):
            water = soil[at, layer, :]
            drained = coef[at, layer, :] * water * water * water
            soil_mid[at, layer, :] = water + coming - drained
            coming = drained
        share = (surface + coming) * (1.0 / SUB)

        down = links[at, :]
        key = (down * W + lane).astype(jnp.float32)
        size = 2
        while size <= W:
            j = size // 2
            while j >= 1:
                other = gat(key, lane ^ j)
                low = ((lane & j) == 0) == ((lane & size) == 0)
                key = jnp.where(low, jnp.minimum(key, other), jnp.maximum(key, other))
                j //= 2
            size *= 2
        key = key.astype(jnp.int32)
        order = key & (W - 1)
        dest = key >> 7
        same = []
        shift = 1
        while shift < W:
            linked = (lane >= shift) & (dest == pltpu.roll(dest, shift, 1))
            same.append((shift, linked.astype(jnp.float32)))
            shift *= 2
        count = jnp.zeros((rows, W), jnp.int32)
        for shift in (64, 32, 16, 8, 4, 2, 1):
            nxt = count + shift
            count = jnp.where(gat(dest, nxt - 1) <= lane, nxt, count)
        end = jnp.maximum(count - 1, 0)
        fed = (count > 0) & (gat(dest, end) == lane)

        s, r = storage[at, :], rate[at, :]
        for n in range(SUB):
            release = r * s
            run = gat(release, order)
            for shift, linked in same:
                run = run + linked * pltpu.roll(run, shift, 1)
            gain = share + jnp.where(fed, gat(run, end), 0.0)
            gains[n, at, :] = gain
            s = s + gain - release
        return 0

    lax.fori_loop(0, CHUNK // rows, body, 0)


def reach_kernel(recv, volume, lag, out):
    got = recv[...]
    turned = jnp.transpose(got)
    lane = iota((W, W), 1)
    total = jnp.zeros((16, W), jnp.float32)
    for c in range(8):
        at = got[:, c * 16 + 10 : c * 16 + 11].astype(jnp.int32)
        hit = (at == lane).astype(jnp.bfloat16)
        for part in split3(turned[c * 16 : c * 16 + 16, :]):
            total += jnp.dot(part, hit, preferred_element_type=jnp.float32)
    row = lambda f: total[f : f + 1, :]
    vol = volume[...]
    back = 1.0 / (1.0 + vol)
    lateral = back * row(0) * (1.0 / W)
    s1 = row(0) - back * row(1) + row(4)
    s2 = row(1) - back * row(2) + row(5)
    s3 = row(2) - back * row(3) + row(6)
    fields = (lag[...], vol, lateral, s1, s2, s3, row(7), row(8), row(9))
    for f, value in enumerate(fields):
        out[:, f * W : (f + 1) * W] = jnp.broadcast_to(value, (W, W))


def shift_rows(x, by, fill):
    return jnp.concatenate([jnp.full((by, W), fill, x.dtype), x[:-by, :]], axis=0)


def finish_kernel(
    me, fields, gains, storage, rate, links, hit, spot, soil_mid, soil_out, storage_out, section, table, flow_ref
):
    lane = iota((W, W), 1)

    @pl.when(pl.program_id(0) == 0)
    def _():
        field = lambda f: fields[:, f * W : (f + 1) * W]
        lag = field(0)
        weight = 1.0 / (1.0 + lag)
        stages = []
        base = weight
        total = weight
        stride = 1
        for radix in (4, 4, 8):
            shifted = [base]
            neutral = total
            gains_of = []
            product = base
            for d in range(1, radix):
                ok = lane >= d * stride
                gains_of.append((d * stride, jnp.where(ok, product, 0.0)))
                moved = pltpu.roll(base, d * stride, 1)
                product = product * moved
                neutral = neutral * jnp.where(ok, pltpu.roll(total, d * stride, 1), 1.0)
            stages.append(gains_of)
            base, total = product, neutral
            stride *= radix
        last = jnp.broadcast_to(total[:, W - 1 : W], (W, W))
        hops = []
        jump = last
        by = 4
        while by < W:
            hops.append((by, jump))
            jump = jump * shift_rows(jump, by, 0.0)
            by *= 2

        volume = field(1)
        lateral = field(2)
        s1, s2, s3 = field(3), field(4), field(5)
        c11, c12, c21 = field(6), field(7), field(8)
        flow = volume
        for n in range(SUB):
            back = 1.0 / (1.0 + volume)
            for part, value in enumerate(split3(back)):
                table[:, (part * SUB + n) * W : (part * SUB + n + 1) * W] = value
            if n == 1:
                lateral = back * s1 * (1.0 / W)
                s1, s2 = s1 - back * s2 + c11, s2 - back * s3 + c12
            elif n == 2:
                lateral = back * s1 * (1.0 / W)
                s1 = s1 - back * s2 + c21
            elif n == 3:
                lateral = back * s1 * (1.0 / W)
            run = weight * (volume + lateral)
            for gains_of in stages:
                add = run
                for d, gain in gains_of:
                    add = add + gain * pltpu.roll(run, d, 1)
                run = add
            head = jnp.broadcast_to(run[:, W - 1 : W], (W, W))
            for by, jump in hops:
                head = head + jump * shift_rows(head, by, 0.0)
            flow = run + total * shift_rows(head, 4, 0.0)
            volume = lag * flow
        flow_ref[...] = flow
        section[...] = jnp.log1p(flow_ref[pl.ds(me[0], 1), :])

    rows = 64
    for half in range(CHUNK // rows):
        at = slice(half * rows, (half + 1) * rows)
        got = jnp.dot(hit[at, :], table[...], preferred_element_type=jnp.float32)
        place = spot[at, :]
        s, r = storage[at, :], rate[at, :]
        leaves = links[at, :] == W
        for n in range(SUB):
            part = lambda k: got[:, (k * SUB + n) * W : (k * SUB + n + 1) * W]
            back = gat(part(0) + part(1) + part(2), place)
            s = s - r * jnp.where(leaves, back, 1.0) * s + gains[n, at, :]
        storage_out[at, :] = s
        top = soil_mid[at, 0, :]
        soil_out[at, 0, :] = top + recharge_share * (s / (s + 1.0)) * (1.0 - top)
        for layer in range(1, 6):
            soil_out[at, layer, :] = soil_mid[at, layer, :]


def local(
    soil_water,
    rainfall,
    drain_coef,
    cell_storage,
    release_rate,
    downstream,
    block_owner,
    outlet_reach,
    river_storage,
    river_lag,
):
    axes = ("tile", "grp")
    blocks = block_owner.shape[0]
    steps = blocks // CHUNK
    layers = soil_water.shape[0]

    def tiles(x):
        return x.reshape(layers, blocks, W).transpose(1, 0, 2)

    soil, coef = tiles(soil_water), tiles(drain_coef)
    rain, storage, rate, links = (
        x.reshape(blocks, W) for x in (rainfall, cell_storage, release_rate, downstream)
    )
    owner = block_owner.reshape(steps, CHUNK)
    reach = outlet_reach.reshape(steps, CHUNK)

    deep = pl.BlockSpec((CHUNK, layers, W), lambda i: (i, 0, 0))
    flat = pl.BlockSpec((CHUNK, W), lambda i: (i, 0))
    four = pl.BlockSpec((SUB, CHUNK, W), lambda i: (0, i, 0))

    def full(*shape):
        return pl.BlockSpec(shape, lambda i: (0,) * len(shape))

    f32 = jnp.float32
    shaped = jax.ShapeDtypeStruct
    params = pltpu.CompilerParams(vmem_limit_bytes=24 * MB)

    send = pl.pallas_call(
        moments_kernel,
        grid=(steps,),
        in_specs=[deep, deep, flat, flat, flat, flat, full(steps, CHUNK), full(steps, CHUNK)],
        out_specs=full(W, W),
        out_shape=shaped((W, W), f32),
        scratch_shapes=[pltpu.VMEM((CHUNK, W), f32), pltpu.VMEM((W, CHUNK), f32)],
        compiler_params=params,
        name="moments",
    )(soil, coef, rain, storage, rate, links, owner, reach)

    recv = lax.all_to_all(send, axes, split_axis=0, concat_axis=0, tiled=True)

    soil_mid, gains, hit, spot = pl.pallas_call(
        inflow_kernel,
        grid=(steps,),
        in_specs=[deep, deep, flat, flat, flat, flat, full(steps, CHUNK), full(steps, CHUNK)],
        out_specs=[deep, four, flat, flat],
        out_shape=[
            shaped((blocks, layers, W), f32),
            shaped((SUB, blocks, W), f32),
            shaped((blocks, W), jnp.bfloat16),
            shaped((blocks, W), jnp.int32),
        ],
        compiler_params=params,
        cost_estimate=pl.CostEstimate(flops=10_000_000, bytes_accessed=16 * MB, transcendentals=0),
        name="inflow",
    )(soil, coef, rain, storage, rate, links, owner, reach)

    fields = pl.pallas_call(
        reach_kernel,
        out_shape=shaped((W, FIELDS * W), f32),
        compiler_params=params,
        name="reaches",
    )(recv, river_storage, river_lag)

    fields = lax.all_to_all(fields, axes, split_axis=0, concat_axis=0, tiled=True)

    me = lax.axis_index(axes).astype(jnp.int32).reshape(1)
    soil_out, storage_out, section = pl.pallas_call(
        finish_kernel,
        grid=(steps,),
        in_specs=[
            pl.BlockSpec(memory_space=pltpu.SMEM),
            full(W, FIELDS * W),
            four,
            flat,
            flat,
            flat,
            flat,
            flat,
            deep,
        ],
        out_specs=[deep, flat, full(1, W)],
        out_shape=[
            shaped((blocks, layers, W), f32),
            shaped((blocks, W), f32),
            shaped((1, W), f32),
        ],
        scratch_shapes=[pltpu.VMEM((W, 3 * SUB * W), jnp.bfloat16), pltpu.VMEM((W, W), f32)],
        compiler_params=params,
        name="finish",
    )(me, fields, gains, storage, rate, links, hit, spot, soil_mid)

    soil_out = soil_out.transpose(1, 0, 2).reshape(layers, blocks * W)
    return (soil_out, storage_out.reshape(-1), section)


def solution(mesh):
    placed = (
        P(None, ("tile", "grp")),
        P(("tile", "grp")),
        P(None, ("tile", "grp")),
        P(("tile", "grp")),
        P(("tile", "grp")),
        P(("tile", "grp")),
        P(("tile", "grp"), None),
        P(("tile", "grp")),
        P("grp", "tile"),
        P("grp", "tile"),
    )
    return jax.shard_map(
        local,
        mesh=mesh,
        in_specs=placed,
        out_specs=(P(None, ("tile", "grp")), P(("tile", "grp")), P("grp", "tile")),
        check_vma=False,
    )
```

```python
import jax
import jax.numpy as jnp
from jax import lax
from jax.experimental import pallas as pl
from jax.experimental.pallas import tpu as pltpu
from jax.sharding import PartitionSpec as P

SUB = 4
recharge_share = 0.2

W = 128
CHUNK = 128
PARTS = 2
FIELDS = 9
MB = 1024 * 1024


def gat(values, index):
    return jnp.take_along_axis(values, index, axis=1, mode="promise_in_bounds")


def iota(shape, dim):
    return lax.broadcasted_iota(jnp.int32, shape, dim)


def split3(x):
    hi = x.astype(jnp.bfloat16)
    rest = x - hi.astype(jnp.float32)
    mid = rest.astype(jnp.bfloat16)
    low = (rest - mid.astype(jnp.float32)).astype(jnp.bfloat16)
    return hi, mid, low


def pick(onehot, x):
    hi, mid, low = split3(x)
    dot = lambda part: jnp.dot(onehot, part, preferred_element_type=jnp.float32)
    return dot(hi) + dot(mid) + dot(low)


def run_all(copies):
    for copy in copies:
        copy.start()
    return copies


def wait_all(copies):
    for copy in copies:
        copy.wait()


def moments_kernel(
    soil, coef, rain, storage, rate, links, owner, reach, send, top, low, low_coef, rain_v, s_v, r_v, to_v, pack_v, sems
):
    lane = iota((W, W), 1)
    sub = iota((W, W), 0)
    steps = owner.shape[0]
    rows = s_v.shape[0] // PARTS
    loads = []
    for part in range(PARTS):
        at = pl.ds(part * rows, rows)
        pairs = (
            (links.at[at], to_v.at[at]),
            (rate.at[at], r_v.at[at]),
            (storage.at[at], s_v.at[at]),
            (rain.at[at], rain_v.at[at]),
            (soil.at[at, 0, :], top.at[at]),
            (soil.at[at, 5, :], low.at[at]),
            (coef.at[at, 5, :], low_coef.at[at]),
        )
        loads.append(
            run_all(
                [
                    pltpu.make_async_copy(src, dst, sems.at[part, k])
                    for k, (src, dst) in enumerate(pairs)
                ]
            )
        )

    before = (sub < lane).astype(jnp.bfloat16)
    hits = []
    carry = jnp.zeros((W, 1), jnp.float32)
    for step in range(steps):
        own = jnp.broadcast_to(owner[step : step + 1, :], (W, CHUNK))
        hit = (own == sub).astype(jnp.float32)
        hit16 = hit.astype(jnp.bfloat16)
        hits.append(hit16)
        seen = jnp.dot(hit16, before, preferred_element_type=jnp.float32) + carry
        carry = carry + jnp.sum(hit, axis=1, keepdims=True)
        rank = jnp.sum(hit * seen, axis=0, keepdims=True)
        both = rank + 8.0 * reach[step : step + 1, :].astype(jnp.float32)
        both = jnp.transpose(jnp.broadcast_to(both, (W, CHUNK)))
        pack_v[step * CHUNK : (step + 1) * CHUNK, :] = both

    for part in range(PARTS):
        at = slice(part * rows, (part + 1) * rows)
        wait_all(loads[part])
        w0, w5 = top[at, :], low[at, :]
        s, r, down = s_v[at, :], r_v[at, :], to_v[at, :]
        share = (rain_v[at, :] * w0 * w0 + low_coef[at, :] * w5 * w5 * w5) * (1.0 / SUB)
        leaves = down == W
        to = down & (W - 1)
        follow = lambda v: jnp.where(leaves, 0.0, gat(v, to))
        a1 = jnp.where(leaves, r, 0.0)
        a2 = a1 * r
        a3 = a2 * r
        g = follow(a1)
        w_1 = r * g
        w_2 = w_1 * g
        w_3 = w_2 * g
        x_1 = r * follow(w_1)
        x_2 = r * follow(w_2)
        z = w_1 * (1.0 - r) + x_1
        y = r * follow(z)
        e1 = (1.0 - r) * s + share
        h1 = a1 * share
        h2 = a2 * share
        terms = (
            a1 * s,
            a2 * s,
            a3 * s,
            a3 * r * s,
            h1 + w_1 * s,
            h2 + w_2 * s,
            a3 * share + w_3 * s,
            h1 + w_1 * e1 + x_1 * s,
            h2 + w_2 * e1 + x_2 * s,
            h1 + w_1 * share + z * e1 + y * s,
        )
        lane_p = iota((rows, W), 1)
        field = lane_p & 15
        both = pack_v[at, :].astype(jnp.int32)
        out = (both >> 3).astype(jnp.float32)
        for f, term in enumerate(terms):
            out = jnp.where(field == f, jnp.sum(term, axis=1, keepdims=True), out)
        pack_v[at, :] = jnp.where((lane_p >> 4) == (both & 7), out, 0.0)

    total = jnp.zeros((W, W), jnp.float32)
    for step in range(steps):
        total = total + pick(hits[step], pack_v[step * CHUNK : (step + 1) * CHUNK, :])
    send[...] = total


def soil_kernel(soil, coef, rain, after, owner, reach, soil_mid, mid0, share, hit, spot, water_v, coef_v, out_v, rain_v, sems, out_sems):
    del after
    layers = water_v.shape[0]
    loads = run_all([pltpu.make_async_copy(rain, rain_v, sems.at[0, layers])])
    for layer in range(layers):
        loads.append(pltpu.make_async_copy(soil.at[:, layer, :], water_v.at[layer], sems.at[0, layer]))
        loads.append(pltpu.make_async_copy(coef.at[:, layer, :], coef_v.at[layer], sems.at[1, layer]))
    run_all(loads[1:])
    sub = iota((W, W), 0)
    for step in range(owner.shape[0]):
        at = slice(step * CHUNK, (step + 1) * CHUNK)
        own = jnp.broadcast_to(owner[step : step + 1, :], (W, CHUNK))
        hit[at, :] = jnp.transpose((own == sub).astype(jnp.float32)).astype(jnp.bfloat16)
        place = jnp.broadcast_to(reach[step : step + 1, :].astype(jnp.float32), (W, CHUNK))
        spot[at, :] = jnp.transpose(place).astype(jnp.int32)
    loads[0].wait()
    stores = []
    coming = surface = None
    for layer in range(layers):
        wait_all(loads[1 + 2 * layer : 3 + 2 * layer])
        water = water_v[layer]
        if layer == 0:
            surface = rain_v[...] * water * water
            coming = rain_v[...] - surface
        drained = coef_v[layer] * water * water * water
        mid = water + coming - drained
        coming = drained
        if layer == 0:
            mid0[...] = mid
        else:
            out_v[layer] = mid
            copy = pltpu.make_async_copy(out_v.at[layer], soil_mid.at[:, layer, :], out_sems.at[layer])
            copy.start()
            stores.append(copy)
    share[...] = (surface + coming) * (1.0 / SUB)
    wait_all(stores)


def inflow_kernel(share, storage, rate, links, gains, key_v, s_v):
    shape = share.shape
    lane = iota(shape, 1)
    key_v[...] = (links[...] * W + lane).astype(jnp.float32)
    size = 2
    while size <= W:
        j = size // 2
        while j >= 1:
            key = key_v[...]
            other = gat(key, lane ^ j)
            low = ((lane & j) == 0) == ((lane & size) == 0)
            key_v[...] = jnp.where(low, jnp.minimum(key, other), jnp.maximum(key, other))
            j //= 2
        size *= 2
    key = key_v[...].astype(jnp.int32)
    order = key & (W - 1)
    dest = key >> 7
    count = jnp.zeros(shape, jnp.int32)
    for shift in (64, 32, 16, 8, 4, 2, 1):
        nxt = count + shift
        count = jnp.where(gat(dest, nxt - 1) <= lane, nxt, count)
    earlier = jnp.where(lane == 0, 0, pltpu.roll(count, 1, 1))
    ahead = (iota((W, W), 0) < iota((W, W), 1)).astype(jnp.bfloat16)
    s_v[...] = storage[...]
    for n in range(SUB):
        s = s_v[...]
        release = rate[...] * s
        run = jnp.zeros(shape, jnp.float32)
        for part in split3(gat(release, order)):
            run = run + jnp.dot(part, ahead, preferred_element_type=jnp.float32)
        gain = share[...] + (gat(run, count) - gat(run, earlier))
        gains[n] = gain
        s_v[...] = s + gain - release


def reach_kernel(recv, volume, lag, out):
    got = recv[...]
    turned = jnp.transpose(got)
    lane = iota((W, W), 1)
    total = jnp.zeros((48, W), jnp.float32)
    for c in range(8):
        at = jnp.broadcast_to(got[:, c * 16 + 10 : c * 16 + 11], (W, W)).astype(jnp.int32)
        hit = (at == lane).astype(jnp.bfloat16)
        parts = jnp.concatenate(split3(turned[c * 16 : c * 16 + 16, :]), axis=0)
        total += jnp.dot(parts, hit, preferred_element_type=jnp.float32)
    total = total[:16, :] + total[16:32, :] + total[32:, :]
    row = lambda f: total[f : f + 1, :]
    vol = volume[...]
    back = 1.0 / (1.0 + vol)
    lateral = back * row(0) * (1.0 / W)
    s1 = row(0) - back * row(1) + row(4)
    s2 = row(1) - back * row(2) + row(5)
    s3 = row(2) - back * row(3) + row(6)
    fields = (lag[...], vol, lateral, s1, s2, s3, row(7), row(8), row(9))
    wide = [jnp.broadcast_to(value, (8, W)) for value in fields]
    sub = iota((8, W), 0)
    period = []
    for k in range(FIELDS):
        tile = jnp.zeros((8, W), jnp.float32)
        for i in range(8):
            tile = jnp.where(sub == i, wide[(k * 8 + i) % FIELDS], tile)
        period.append(tile)
    for k in range(W // 8):
        for f in range(FIELDS):
            at = (k * FIELDS + f) * 8
            out[at : at + 8, :] = period[f]


def shift_rows(x, by, fill):
    return jnp.concatenate([jnp.full((by, W), fill, x.dtype), x[:-by, :]], axis=0)


def finish_kernel(
    me, fields, gains, storage, rate, links, hit, spot, mid0, soil_mid, soil_out, storage_out, section,
    table, flow_ref, g_v, s_v, r_v, to_v, hit_v, spot_v, mid_v, out_v, top_v, sems, out_sems
):
    del soil_mid
    lane = iota((W, W), 1)
    loads = run_all(
        [
            pltpu.make_async_copy(src, dst, sems.at[k])
            for k, (src, dst) in enumerate(
                (
                    (hit, hit_v),
                    (spot, spot_v),
                    (storage, s_v),
                    (rate, r_v),
                    (links, to_v),
                    (gains, g_v),
                    (mid0, mid_v),
                )
            )
        ]
    )
    field = lambda f: fields[pl.ds(f, W, FIELDS), :]
    lag = field(0)
    weight = 1.0 / (1.0 + lag)
    stages = []
    base = weight
    total = weight
    stride = 1
    for radix in (4, 4, 8):
        neutral = total
        gains_of = []
        product = base
        for d in range(1, radix):
            ok = lane >= d * stride
            gains_of.append((d * stride, jnp.where(ok, product, 0.0)))
            product = product * pltpu.roll(base, d * stride, 1)
            neutral = neutral * jnp.where(ok, pltpu.roll(total, d * stride, 1), 1.0)
        stages.append(gains_of)
        base, total = product, neutral
        stride *= radix
    last = jnp.broadcast_to(total[:, W - 1 : W], (W, W))
    hops = []
    jump = last
    by = 4
    while by < W:
        hops.append((by, jump))
        jump = jump * shift_rows(jump, by, 0.0)
        by *= 2

    volume = field(1)
    lateral = field(2)
    s1, s2, s3 = field(3), field(4), field(5)
    c11, c12, c21 = field(6), field(7), field(8)
    flow = volume
    for n in range(SUB):
        back = 1.0 / (1.0 + volume)
        for part, value in enumerate(split3(back)):
            table[:, (part * SUB + n) * W : (part * SUB + n + 1) * W] = value
        if n == 1:
            lateral = back * s1 * (1.0 / W)
            s1, s2 = s1 - back * s2 + c11, s2 - back * s3 + c12
        elif n == 2:
            lateral = back * s1 * (1.0 / W)
            s1 = s1 - back * s2 + c21
        elif n == 3:
            lateral = back * s1 * (1.0 / W)
        run = weight * (volume + lateral)
        for gains_of in stages:
            add = run
            for d, gain in gains_of:
                add = add + gain * pltpu.roll(run, d, 1)
            run = add
        head = jnp.broadcast_to(run[:, W - 1 : W], (W, W))
        for by, jump in hops:
            head = head + jump * shift_rows(head, by, 0.0)
        flow = run + total * shift_rows(head, 4, 0.0)
        volume = lag * flow
    flow_ref[...] = flow
    section[...] = jnp.log1p(flow_ref[pl.ds(me[0], 1), :])

    wait_all(loads)
    stores = []
    blocks = s_v.shape[0]
    for step in range(blocks // CHUNK):
        at = slice(step * CHUNK, (step + 1) * CHUNK)
        got = jnp.dot(hit_v[at, :], table[...], preferred_element_type=jnp.float32)
        place = spot_v[at, :]
        s, r = s_v[at, :], r_v[at, :]
        leaves = to_v[at, :] == W
        for n in range(SUB):
            part = lambda k: got[:, (k * SUB + n) * W : (k * SUB + n + 1) * W]
            back = gat(part(0) + part(1) + part(2), place)
            s = s - r * jnp.where(leaves, back, 1.0) * s + g_v[n, at, :]
        out_v[at, :] = s
        top = mid_v[at, :]
        top_v[at, :] = top + recharge_share * (s / (s + 1.0)) * (1.0 - top)
        where = pl.ds(step * CHUNK, CHUNK)
        stores += run_all(
            [
                pltpu.make_async_copy(out_v.at[where], storage_out.at[where], out_sems.at[0, step]),
                pltpu.make_async_copy(top_v.at[where], soil_out.at[where, 0, :], out_sems.at[1, step]),
            ]
        )
    wait_all(stores)


def local(
    soil_water,
    rainfall,
    drain_coef,
    cell_storage,
    release_rate,
    downstream,
    block_owner,
    outlet_reach,
    river_storage,
    river_lag,
):
    axes = ("tile", "grp")
    blocks = block_owner.shape[0]
    steps = blocks // CHUNK
    layers = soil_water.shape[0]

    def tiles(x):
        return x.reshape(layers, blocks, W).transpose(1, 0, 2)

    soil, coef = tiles(soil_water), tiles(drain_coef)
    rain, storage, rate, links = (
        x.reshape(blocks, W) for x in (rainfall, cell_storage, release_rate, downstream)
    )
    owner = block_owner.reshape(steps, CHUNK)
    reach = outlet_reach.reshape(steps, CHUNK)

    f32 = jnp.float32
    i32 = jnp.int32
    b16 = jnp.bfloat16
    shaped = jax.ShapeDtypeStruct
    vmem = pl.BlockSpec(memory_space=pltpu.VMEM)
    hbm = pl.BlockSpec(memory_space=pltpu.HBM)
    params = pltpu.CompilerParams(vmem_limit_bytes=24 * MB)
    alone = pltpu.CompilerParams(vmem_limit_bytes=60 * MB)
    scratch = lambda dtype, *shape: pltpu.VMEM(shape, dtype)
    flat = lambda dtype: scratch(dtype, blocks, W)
    sems = lambda *shape: pltpu.SemaphoreType.DMA(shape)
    cost = lambda flops, moved: pl.CostEstimate(flops=flops, bytes_accessed=moved, transcendentals=0)

    send = pl.pallas_call(
        moments_kernel,
        in_specs=[hbm] * 6 + [vmem] * 2,
        out_specs=vmem,
        out_shape=shaped((W, W), f32),
        scratch_shapes=[flat(f32)] * 6 + [flat(i32), flat(f32), sems(PARTS, 7)],
        compiler_params=alone,
        name="moments",
    )(soil, coef, rain, storage, rate, links, owner, reach)

    recv = lax.all_to_all(send, axes, split_axis=0, concat_axis=0, tiled=True)

    soil_mid, mid0, share, hit, spot = pl.pallas_call(
        soil_kernel,
        in_specs=[hbm] * 4 + [vmem] * 2,
        out_specs=[hbm] + [vmem] * 4,
        out_shape=[
            shaped((blocks, layers, W), f32),
            shaped((blocks, W), f32),
            shaped((blocks, W), f32),
            shaped((blocks, W), b16),
            shaped((blocks, W), i32),
        ],
        scratch_shapes=[scratch(f32, layers, blocks, W)] * 3 + [flat(f32), sems(2, layers + 1), sems(layers)],
        compiler_params=alone,
        cost_estimate=cost(3_000_000, 10 * MB),
        name="soil",
    )(soil, coef, rain, send, owner, reach)

    recv, share = lax.optimization_barrier((recv, share))

    gains = pl.pallas_call(
        inflow_kernel,
        in_specs=[vmem] * 4,
        out_specs=vmem,
        out_shape=shaped((SUB, blocks, W), f32),
        scratch_shapes=[flat(f32)] * 2,
        compiler_params=params,
        cost_estimate=cost(10_000_000, 16 * MB),
        name="inflow",
    )(share, storage, rate, links)

    fields = pl.pallas_call(
        reach_kernel,
        in_specs=[vmem] * 3,
        out_specs=vmem,
        out_shape=shaped((W * FIELDS, W), f32),
        compiler_params=params,
        name="reaches",
    )(recv, river_storage, river_lag)

    fields = fields.reshape(W, 1, FIELDS * W)
    fields = lax.all_to_all(fields, axes, split_axis=0, concat_axis=0, tiled=True)
    fields = fields.reshape(W * FIELDS, W)

    me = lax.axis_index(axes).astype(jnp.int32).reshape(1)
    soil_out, storage_out, section = pl.pallas_call(
        finish_kernel,
        in_specs=[pl.BlockSpec(memory_space=pltpu.SMEM), vmem] + [hbm] * 8,
        out_specs=[hbm, hbm, vmem],
        out_shape=[
            shaped((blocks, layers, W), f32),
            shaped((blocks, W), f32),
            shaped((1, W), f32),
        ],
        scratch_shapes=[
            scratch(b16, W, 3 * SUB * W),
            scratch(f32, W, W),
            scratch(f32, SUB, blocks, W),
            flat(f32),
            flat(f32),
            flat(i32),
            flat(b16),
            flat(i32),
            flat(f32),
            flat(f32),
            flat(f32),
            sems(7),
            sems(2, steps),
        ],
        input_output_aliases={9: 0},
        compiler_params=params,
        name="finish",
    )(me, fields, gains, storage, rate, links, hit, spot, mid0, soil_mid)

    soil_out = soil_out.transpose(1, 0, 2).reshape(layers, blocks * W)
    return (soil_out, storage_out.reshape(-1), section)


def solution(mesh):
    placed = (
        P(None, ("tile", "grp")),
        P(("tile", "grp")),
        P(None, ("tile", "grp")),
        P(("tile", "grp")),
        P(("tile", "grp")),
        P(("tile", "grp")),
        P(("tile", "grp"), None),
        P(("tile", "grp")),
        P("grp", "tile"),
        P("grp", "tile"),
    )
    return jax.shard_map(
        local,
        mesh=mesh,
        in_specs=placed,
        out_specs=(P(None, ("tile", "grp")), P(("tile", "grp")), P("grp", "tile")),
        check_vma=False,
    )
```

```python
import jax
import jax.numpy as jnp
from jax import lax
from jax.experimental import pallas as pl
from jax.experimental.pallas import tpu as pltpu
from jax.sharding import PartitionSpec as P

SUB = 4
RIVERS = 4
recharge_share = 0.2

W = 128
CHUNK = 128
AHEAD = 3
FIELDS = 7
MB = 1024 * 1024


def gat(values, index):
    return jnp.take_along_axis(values, index, axis=1, mode="promise_in_bounds")


def iota(shape, dim):
    return lax.broadcasted_iota(jnp.int32, shape, dim)


def split3(x):
    hi = x.astype(jnp.bfloat16)
    rest = x - hi.astype(jnp.float32)
    mid = rest.astype(jnp.bfloat16)
    low = (rest - mid.astype(jnp.float32)).astype(jnp.bfloat16)
    return hi, mid, low


def run_all(copies):
    for copy in copies:
        copy.start()
    return copies


def wait_all(copies):
    for copy in copies:
        copy.wait()


def moments_kernel(
    soil, coef, rain, storage, rate, links, owner, reach, volume, lag, send, top, low, low_coef, rain_v, s_v, r_v, to_v, pack_v, sems
):
    lane = iota((W, W), 1)
    sub = iota((W, W), 0)
    pairs = (
        (links, to_v),
        (rate, r_v),
        (storage, s_v),
        (soil.at[:, 0, :], top),
        (soil.at[:, 5, :], low),
        (coef.at[:, 5, :], low_coef),
        (rain, rain_v),
    )
    loads = run_all([pltpu.make_async_copy(src, dst, sems.at[k]) for k, (src, dst) in enumerate(pairs)])

    before = (sub < lane).astype(jnp.bfloat16)
    hits = []
    carry = jnp.zeros((W, 1), jnp.float32)
    for step in range(owner.shape[0]):
        own = jnp.broadcast_to(owner[step : step + 1, :], (W, CHUNK))
        hit = (own == sub).astype(jnp.float32)
        hit16 = hit.astype(jnp.bfloat16)
        hits.append(hit16)
        seen = jnp.dot(hit16, before, preferred_element_type=jnp.float32) + carry
        carry = carry + jnp.sum(hit, axis=1, keepdims=True)
        rank = jnp.sum(hit * seen, axis=0, keepdims=True)
        both = rank + 8.0 * reach[step : step + 1, :].astype(jnp.float32)
        both = jnp.transpose(jnp.broadcast_to(both, (W, CHUNK)))
        pack_v[step * CHUNK : (step + 1) * CHUNK, :] = both
    send[pl.ds(1, W, AHEAD), :] = jnp.broadcast_to(lag[...], (W, W))
    send[pl.ds(2, W, AHEAD), :] = jnp.broadcast_to(volume[...], (W, W))

    field = iota(s_v.shape, 1) & 15
    slot = iota(s_v.shape, 1) >> 4
    both = pack_v[...].astype(jnp.int32)
    out = (both >> 3).astype(jnp.float32)
    total = lambda term: jnp.sum(term, axis=1, keepdims=True)

    wait_all(loads[:2])
    r, down = r_v[...], to_v[...]
    leaves = down == W
    to = down & (W - 1)
    follow = lambda v: jnp.where(leaves, 0.0, gat(v, to))
    a1 = jnp.where(leaves, r, 0.0)
    a2 = a1 * r
    a3 = a2 * r
    g = follow(a1)
    w_1 = r * g
    w_2 = w_1 * g
    w_3 = w_2 * g
    x_1 = r * follow(w_1)
    x_2 = r * follow(w_2)
    z = w_1 * (1.0 - r) + x_1
    y = r * follow(z)
    loads[2].wait()
    s = s_v[...]
    for f, a in enumerate((a1, a2, a3, a3 * r)):
        out = jnp.where(field == f, total(a * s), out)
    wait_all(loads[3:])
    w0, w5 = top[...], low[...]
    share = (rain_v[...] * w0 * w0 + low_coef[...] * w5 * w5 * w5) * (1.0 / SUB)
    e1 = (1.0 - r) * s + share
    h1 = a1 * share
    h2 = a2 * share
    terms = (
        h1 + w_1 * s,
        h2 + w_2 * s,
        a3 * share + w_3 * s,
        h1 + w_1 * e1 + x_1 * s,
        h2 + w_2 * e1 + x_2 * s,
        h1 + w_1 * share + z * e1 + y * s,
    )
    for f, term in enumerate(terms):
        out = jnp.where(field == f + 4, total(term), out)
    out = jnp.where(slot == (both & 7), out, 0.0)
    parts = jnp.concatenate(split3(out), axis=1)
    got = jnp.dot(jnp.concatenate(hits, axis=1), parts, preferred_element_type=jnp.float32)
    send[pl.ds(0, W, AHEAD), :] = got[:, :W] + got[:, W : 2 * W] + got[:, 2 * W :]


def soil_kernel(soil, coef, rain, after, owner, reach, soil_mid, mid0, share, hit, spot, water_v, coef_v, out_v, rain_v, sems, out_sems):
    del after
    layers = water_v.shape[0]
    loads = run_all([pltpu.make_async_copy(rain, rain_v, sems.at[0, layers])])
    for layer in range(layers):
        loads.append(pltpu.make_async_copy(soil.at[:, layer, :], water_v.at[layer], sems.at[0, layer]))
        loads.append(pltpu.make_async_copy(coef.at[:, layer, :], coef_v.at[layer], sems.at[1, layer]))
    run_all(loads[1:])
    sub = iota((W, W), 0)
    for step in range(owner.shape[0]):
        at = slice(step * CHUNK, (step + 1) * CHUNK)
        at_reach = jnp.broadcast_to(reach[step : step + 1, :], (W, CHUNK))
        hit[at, :] = jnp.transpose((at_reach == sub).astype(jnp.float32)).astype(jnp.bfloat16)
        place = jnp.broadcast_to(owner[step : step + 1, :].astype(jnp.float32), (W, CHUNK))
        spot[at, :] = jnp.transpose(place).astype(jnp.int32)
    loads[0].wait()
    stores = []
    coming = surface = None
    for layer in range(layers):
        wait_all(loads[1 + 2 * layer : 3 + 2 * layer])
        water = water_v[layer]
        if layer == 0:
            surface = rain_v[...] * water * water
            coming = rain_v[...] - surface
        drained = coef_v[layer] * water * water * water
        mid = water + coming - drained
        coming = drained
        if layer == 0:
            mid0[...] = mid
        else:
            out_v[layer] = mid
            copy = pltpu.make_async_copy(out_v.at[layer], soil_mid.at[:, layer, :], out_sems.at[layer])
            copy.start()
            stores.append(copy)
    share[...] = (surface + coming) * (1.0 / SUB)
    wait_all(stores)


def sort_columns(v):
    sub = iota((8, W), 0)
    size = 2
    while size <= W:
        j = size // 2
        while j >= 1:
            for a in range(16):
                if j >= 16:
                    d = j >> 4
                    clear = (sub & d) == 0
                    other = jnp.where(clear, pltpu.roll(v[a], 8 - d, 0), pltpu.roll(v[a], d, 0))
                    bit = sub // d & 1
                    lower = bit == (sub // (size >> 4) & 1) if size < W else clear
                    v[a] = jnp.where(lower, jnp.minimum(v[a], other), jnp.maximum(v[a], other))
                elif not a & j:
                    b = a | j
                    low, high = jnp.minimum(v[a], v[b]), jnp.maximum(v[a], v[b])
                    if size < 16:
                        v[a], v[b] = (high, low) if a & size else (low, high)
                    elif size == W:
                        v[a], v[b] = low, high
                    else:
                        up = (sub & (size >> 4)) == 0
                        v[a], v[b] = jnp.where(up, low, high), jnp.where(up, high, low)
            j //= 2
        size *= 2
    return v


def river_tables(recv, tables):
    lag = jnp.transpose(recv[pl.ds(1, W, AHEAD), :])
    volume = jnp.transpose(recv[pl.ds(2, W, AHEAD), :])
    row = iota((W, W), 0)
    weight = 1.0 / (1.0 + lag)
    product = prefix = suffix = weight
    by = 1
    k = 0
    while by < W:
        ok = row >= by
        tables[k] = jnp.where(ok, product, 0.0)
        product = product * pltpu.roll(product, by, 0)
        prefix = prefix * jnp.where(ok, pltpu.roll(prefix, by, 0), 1.0)
        suffix = suffix * jnp.where(row < W - by, pltpu.roll(suffix, W - by, 0), 1.0)
        by *= 2
        k += 1
    for i, value in enumerate((prefix, suffix, weight, lag, volume)):
        tables[k + i] = value
    whole = jnp.transpose(jnp.broadcast_to(prefix[W - 1 : W, :], (W, W)))
    factor = jnp.where(row < W - RIVERS, pltpu.roll(whole, W - RIVERS, 0), 0.0)
    reached = (iota((W, W), 1) == row + RIVERS).astype(jnp.float32)
    by = RIVERS
    while by < W:
        reached = reached + factor * pltpu.roll(reached, W - by, 0)
        factor = factor * pltpu.roll(factor, W - by, 0)
        by *= 2
    for i, part in enumerate(split3(reached)):
        tables[k + 5 + i] = part.astype(jnp.float32)


def inflow_kernel(share, storage, rate, links, recv, gains, tables, key_v, s_v, share_v, sem):
    load = pltpu.make_async_copy(share, share_v, sem)
    load.start()
    shape = storage.shape
    sub = iota((8, W), 0)
    for step in range(shape[0] // CHUNK):
        at = slice(step * CHUNK, (step + 1) * CHUNK)
        turned = jnp.transpose(links[at, :].astype(jnp.float32))
        tiles = [
            turned[8 * a : 8 * a + 8, :] * float(W) + (sub + 8 * a).astype(jnp.float32)
            for a in range(W // 8)
        ]
        key_v[at, :] = jnp.transpose(jnp.concatenate(sort_columns(tiles), axis=0))
    river_tables(recv, tables)

    lane = iota(shape, 1)
    key = key_v[...].astype(jnp.int32)
    order = key & (W - 1)
    dest = key >> 7
    count = jnp.zeros(shape, jnp.int32)
    for shift in (64, 32, 16, 8, 4, 2, 1):
        last = count + (shift - 1)
        found = gat(dest, ((last & 15) << 3) | (last >> 4))
        count = jnp.where(found <= lane, count + shift, count)
    earlier = jnp.where(lane == 0, 0, pltpu.roll(count, 1, 1))
    q = iota((W, W), 0)
    ahead = ((q >> 3) + 16 * (q & 7) < iota((W, W), 1)).astype(jnp.bfloat16)
    ahead = jnp.concatenate([ahead] * 3, axis=0)
    s_v[...] = storage[...]
    load.wait()
    for n in range(SUB):
        s = s_v[...]
        release = rate[...] * s
        parts = jnp.concatenate(split3(gat(release, order)), axis=1)
        run = jnp.dot(parts, ahead, preferred_element_type=jnp.float32)
        gain = share_v[...] + (gat(run, count) - gat(run, earlier))
        gains[n] = gain
        s_v[...] = s + gain - release


def reach_kernel(recv, volume, out):
    got = recv[pl.ds(0, W, AHEAD), :]
    turned = jnp.transpose(got)
    lane = iota((W, W), 1)
    total = jnp.zeros((48, W), jnp.float32)
    for c in range(8):
        at = jnp.broadcast_to(got[:, c * 16 + 10 : c * 16 + 11], (W, W)).astype(jnp.int32)
        hit = (at == lane).astype(jnp.bfloat16)
        parts = jnp.concatenate(split3(turned[c * 16 : c * 16 + 16, :]), axis=0)
        total += jnp.dot(parts, hit, preferred_element_type=jnp.float32)
    total = total[:16, :] + total[16:32, :] + total[32:, :]
    row = lambda f: total[f : f + 1, :]
    vol = volume[...]
    back = 1.0 / (1.0 + vol)
    lateral = back * row(0) * (1.0 / W)
    s1 = row(0) - back * row(1) + row(4)
    s2 = row(1) - back * row(2) + row(5)
    s3 = row(2) - back * row(3) + row(6)
    fields = (lateral, s1, s2, s3, row(7), row(8), row(9))
    wide = [jnp.broadcast_to(value, (8, W)) for value in fields]
    sub = iota((8, W), 0)
    period = []
    for k in range(FIELDS):
        tile = jnp.zeros((8, W), jnp.float32)
        for i in range(8):
            tile = jnp.where(sub == i, wide[(k * 8 + i) % FIELDS], tile)
        period.append(tile)
    for k in range(W // 8):
        for f in range(FIELDS):
            at = (k * FIELDS + f) * 8
            out[at : at + 8, :] = period[f]


def finish_kernel(
    me, fields, tables, gains, storage, rate, links, hit, spot, mid0, soil_mid, soil_out, storage_out, section,
    table, flow_ref, g_v, s_v, r_v, to_v, hit_v, spot_v, mid_v, out_v, top_v, sems, out_sems
):
    del soil_mid
    loads = run_all(
        [
            pltpu.make_async_copy(src, dst, sems.at[k])
            for k, (src, dst) in enumerate(
                (
                    (hit, hit_v),
                    (spot, spot_v),
                    (storage, s_v),
                    (rate, r_v),
                    (links, to_v),
                    (gains, g_v),
                    (mid0, mid_v),
                )
            )
        ]
    )
    field = lambda f: jnp.transpose(fields[pl.ds(f, W, FIELDS), :])
    levels = 7
    prefix, suffix, weight, lag, volume = (tables[levels + k] for k in range(5))
    crossing = jnp.concatenate([tables[levels + 5 + k].astype(jnp.bfloat16) for k in range(3)], axis=1)
    lateral = field(0)
    s1, s2, s3 = field(1), field(2), field(3)
    c11, c12, c21 = field(4), field(5), field(6)
    flow = volume
    for n in range(SUB):
        back = 1.0 / (1.0 + volume)
        for part, value in enumerate(split3(back)):
            table[:, (part * SUB + n) * W : (part * SUB + n + 1) * W] = value
        if n == 1:
            lateral = back * s1 * (1.0 / W)
            s1, s2 = s1 - back * s2 + c11, s2 - back * s3 + c12
        elif n == 2:
            lateral = back * s1 * (1.0 / W)
            s1 = s1 - back * s2 + c21
        elif n == 3:
            lateral = back * s1 * (1.0 / W)
        entering = volume + lateral
        ends = jnp.sum(entering * suffix, axis=0, keepdims=True)
        ends = jnp.concatenate([jnp.broadcast_to(part, (16, W)) for part in split3(ends)], axis=0)
        head = jnp.dot(ends, crossing, preferred_element_type=jnp.float32)
        head = head[:8, :] + head[16:24, :] + head[32:40, :]
        head = head[:1, :W] + head[:1, W : 2 * W] + head[:1, 2 * W :]
        run = weight * entering
        for k in range(levels):
            run = run + tables[k] * pltpu.roll(run, 1 << k, 0)
        flow = run + prefix * head
        volume = lag * flow
    flow_ref[...] = jnp.transpose(flow)
    section[...] = jnp.log1p(flow_ref[pl.ds(me[0], 1), :])

    wait_all(loads)
    stores = []
    blocks = s_v.shape[0]
    for step in range(blocks // CHUNK):
        at = slice(step * CHUNK, (step + 1) * CHUNK)
        got = jnp.dot(hit_v[at, :], table[...], preferred_element_type=jnp.float32)
        place = spot_v[at, :]
        s, r = s_v[at, :], r_v[at, :]
        leaves = to_v[at, :] == W
        for n in range(SUB):
            part = lambda k: got[:, (k * SUB + n) * W : (k * SUB + n + 1) * W]
            back = gat(part(0) + part(1) + part(2), place)
            s = s - r * jnp.where(leaves, back, 1.0) * s + g_v[n, at, :]
        out_v[at, :] = s
        top = mid_v[at, :]
        top_v[at, :] = top + recharge_share * (s / (s + 1.0)) * (1.0 - top)
        where = pl.ds(step * CHUNK, CHUNK)
        stores += run_all(
            [
                pltpu.make_async_copy(out_v.at[where], storage_out.at[where], out_sems.at[0, step]),
                pltpu.make_async_copy(top_v.at[where], soil_out.at[where, 0, :], out_sems.at[1, step]),
            ]
        )
    wait_all(stores)


def local(
    soil_water,
    rainfall,
    drain_coef,
    cell_storage,
    release_rate,
    downstream,
    block_owner,
    outlet_reach,
    river_storage,
    river_lag,
):
    axes = ("tile", "grp")
    blocks = block_owner.shape[0]
    steps = blocks // CHUNK
    layers = soil_water.shape[0]

    def tiles(x):
        return x.reshape(layers, blocks, W).transpose(1, 0, 2)

    soil, coef = tiles(soil_water), tiles(drain_coef)
    rain, storage, rate, links = (
        x.reshape(blocks, W) for x in (rainfall, cell_storage, release_rate, downstream)
    )
    owner = block_owner.reshape(steps, CHUNK)
    reach = outlet_reach.reshape(steps, CHUNK)

    f32 = jnp.float32
    i32 = jnp.int32
    b16 = jnp.bfloat16
    shaped = jax.ShapeDtypeStruct
    vmem = pl.BlockSpec(memory_space=pltpu.VMEM)
    hbm = pl.BlockSpec(memory_space=pltpu.HBM)
    params = pltpu.CompilerParams(vmem_limit_bytes=24 * MB)
    scratch = lambda dtype, *shape: pltpu.VMEM(shape, dtype)
    flat = lambda dtype: scratch(dtype, blocks, W)
    stay = lambda x: pltpu.with_memory_space_constraint(x, pltpu.HBM)
    sems = lambda *shape: pltpu.SemaphoreType.DMA(shape)
    cost = lambda flops, moved: pl.CostEstimate(flops=flops, bytes_accessed=moved, transcendentals=0)

    send = pl.pallas_call(
        moments_kernel,
        in_specs=[hbm] * 6 + [vmem] * 4,
        out_specs=vmem,
        out_shape=shaped((W * AHEAD, W), f32),
        scratch_shapes=[flat(f32)] * 6 + [flat(i32), flat(f32), sems(7)],
        compiler_params=params,
        name="moments",
    )(*map(stay, (soil, coef, rain, storage, rate, links, owner, reach, river_storage, river_lag)))

    def exchange(rows, count):
        rows = rows.reshape(W, 1, count * W)
        rows = lax.all_to_all(rows, axes, split_axis=0, concat_axis=0, tiled=True)
        return rows.reshape(W * count, W)

    recv = exchange(send, AHEAD)

    soil_mid, mid0, share, hit, spot = pl.pallas_call(
        soil_kernel,
        in_specs=[hbm] * 4 + [vmem] * 2,
        out_specs=[hbm] + [vmem] * 4,
        out_shape=[
            pltpu.HBM((blocks, layers, W), f32),
            pltpu.HBM((blocks, W), f32),
            pltpu.HBM((blocks, W), f32),
            pltpu.HBM((blocks, W), b16),
            pltpu.HBM((blocks, W), i32),
        ],
        scratch_shapes=[scratch(f32, layers, blocks, W)] * 3 + [flat(f32), sems(2, layers + 1), sems(layers)],
        compiler_params=params,
        cost_estimate=cost(3_000_000, 10 * MB),
        name="soil",
    )(*map(stay, (soil, coef, rain, send, owner, reach)))

    recv, spot = lax.optimization_barrier((recv, spot))

    fields = pl.pallas_call(
        reach_kernel,
        in_specs=[vmem] * 2,
        out_specs=vmem,
        out_shape=shaped((W * FIELDS, W), f32),
        compiler_params=params,
        name="reaches",
    )(recv, river_storage)
    fields, recv = lax.optimization_barrier((fields, recv))
    fields = exchange(fields, FIELDS)

    gains, tables = pl.pallas_call(
        inflow_kernel,
        in_specs=[hbm] + [vmem] * 4,
        out_specs=[vmem] * 2,
        out_shape=[shaped((SUB, blocks, W), f32), shaped((15, W, W), f32)],
        scratch_shapes=[flat(f32)] * 3 + [pltpu.SemaphoreType.DMA],
        compiler_params=params,
        cost_estimate=cost(10_000_000, 16 * MB),
        name="inflow",
    )(stay(share), storage, rate, links, recv)

    me = lax.axis_index(axes).astype(jnp.int32).reshape(1)
    soil_out, storage_out, section = pl.pallas_call(
        finish_kernel,
        in_specs=[pl.BlockSpec(memory_space=pltpu.SMEM)] + [vmem] * 2 + [hbm] * 8,
        out_specs=[hbm, hbm, vmem],
        out_shape=[
            shaped((blocks, layers, W), f32),
            shaped((blocks, W), f32),
            shaped((1, W), f32),
        ],
        scratch_shapes=[
            scratch(b16, W, 3 * SUB * W),
            scratch(f32, W, W),
            scratch(f32, SUB, blocks, W),
            flat(f32),
            flat(f32),
            flat(i32),
            flat(b16),
            flat(i32),
            flat(f32),
            flat(f32),
            flat(f32),
            sems(7),
            sems(2, steps),
        ],
        input_output_aliases={10: 0},
        compiler_params=params,
        name="finish",
    )(me, fields, tables, gains, *map(stay, (storage, rate, links, hit, spot, mid0, soil_mid)))

    soil_out = soil_out.transpose(1, 0, 2).reshape(layers, blocks * W)
    return (soil_out, storage_out.reshape(-1), section)


def solution(mesh):
    placed = (
        P(None, ("tile", "grp")),
        P(("tile", "grp")),
        P(None, ("tile", "grp")),
        P(("tile", "grp")),
        P(("tile", "grp")),
        P(("tile", "grp")),
        P(("tile", "grp"), None),
        P(("tile", "grp")),
        P("grp", "tile"),
        P("grp", "tile"),
    )
    return jax.shard_map(
        local,
        mesh=mesh,
        in_specs=placed,
        out_specs=(P(None, ("tile", "grp")), P(("tile", "grp")), P("grp", "tile")),
        check_vma=False,
    )
```

```python
import jax
import jax.numpy as jnp
from jax import lax
from jax.experimental import pallas as pl
from jax.experimental.pallas import tpu as pltpu
from jax.sharding import PartitionSpec as P

SUB = 4
RIVERS = 4
recharge_share = 0.2

W = 128
CHUNK = 128
AHEAD = 3
FIELDS = 7
MB = 1024 * 1024


def gat(values, index):
    return jnp.take_along_axis(values, index, axis=1, mode="promise_in_bounds")


def iota(shape, dim):
    return lax.broadcasted_iota(jnp.int32, shape, dim)


def split3(x):
    hi = x.astype(jnp.bfloat16)
    rest = x - hi.astype(jnp.float32)
    mid = rest.astype(jnp.bfloat16)
    low = (rest - mid.astype(jnp.float32)).astype(jnp.bfloat16)
    return hi, mid, low


def run_all(copies):
    for copy in copies:
        copy.start()
    return copies


def wait_all(copies):
    for copy in copies:
        copy.wait()


def moments_kernel(
    soil, coef, rain, storage, rate, links, owner_hbm, reach_hbm, volume_hbm, lag_hbm, send,
    top, low, low_coef, rain_v, s_v, r_v, to_v, pack_v, owner, reach, volume, lag, sems
):
    lane = iota((W, W), 1)
    sub = iota((W, W), 0)
    pairs = (
        (owner_hbm, owner),
        (reach_hbm, reach),
        (volume_hbm, volume),
        (lag_hbm, lag),
        (links, to_v),
        (rate, r_v),
        (storage, s_v),
        (soil.at[:, 0, :], top),
        (soil.at[:, 5, :], low),
        (coef.at[:, 5, :], low_coef),
        (rain, rain_v),
    )
    loads = run_all([pltpu.make_async_copy(src, dst, sems.at[k]) for k, (src, dst) in enumerate(pairs)])

    small, loads = loads[:4], loads[4:]
    wait_all(small)
    before = (sub < lane).astype(jnp.bfloat16)
    hits = []
    carry = jnp.zeros((W, 1), jnp.float32)
    for step in range(owner.shape[0]):
        own = jnp.broadcast_to(owner[step : step + 1, :], (W, CHUNK))
        hit = (own == sub).astype(jnp.float32)
        hit16 = hit.astype(jnp.bfloat16)
        hits.append(hit16)
        seen = jnp.dot(hit16, before, preferred_element_type=jnp.float32) + carry
        carry = carry + jnp.sum(hit, axis=1, keepdims=True)
        rank = jnp.sum(hit * seen, axis=0, keepdims=True)
        both = rank + 8.0 * reach[step : step + 1, :].astype(jnp.float32)
        both = jnp.transpose(jnp.broadcast_to(both, (W, CHUNK)))
        pack_v[step * CHUNK : (step + 1) * CHUNK, :] = both
    send[pl.ds(1, W, AHEAD), :] = jnp.broadcast_to(lag[...], (W, W))
    send[pl.ds(2, W, AHEAD), :] = jnp.broadcast_to(volume[...], (W, W))

    field = iota(s_v.shape, 1) & 15
    slot = iota(s_v.shape, 1) >> 4
    both = pack_v[...].astype(jnp.int32)
    out = (both >> 3).astype(jnp.float32)
    total = lambda term: jnp.sum(term, axis=1, keepdims=True)

    wait_all(loads[:2])
    r, down = r_v[...], to_v[...]
    leaves = down == W
    to = down & (W - 1)
    follow = lambda v: jnp.where(leaves, 0.0, gat(v, to))
    a1 = jnp.where(leaves, r, 0.0)
    a2 = a1 * r
    a3 = a2 * r
    g = follow(a1)
    w_1 = r * g
    w_2 = w_1 * g
    w_3 = w_2 * g
    x_1 = r * follow(w_1)
    x_2 = r * follow(w_2)
    z = w_1 * (1.0 - r) + x_1
    y = r * follow(z)
    loads[2].wait()
    s = s_v[...]
    for f, a in enumerate((a1, a2, a3, a3 * r)):
        out = jnp.where(field == f, total(a * s), out)
    wait_all(loads[3:])
    w0, w5 = top[...], low[...]
    share = (rain_v[...] * w0 * w0 + low_coef[...] * w5 * w5 * w5) * (1.0 / SUB)
    e1 = (1.0 - r) * s + share
    h1 = a1 * share
    h2 = a2 * share
    terms = (
        h1 + w_1 * s,
        h2 + w_2 * s,
        a3 * share + w_3 * s,
        h1 + w_1 * e1 + x_1 * s,
        h2 + w_2 * e1 + x_2 * s,
        h1 + w_1 * share + z * e1 + y * s,
    )
    for f, term in enumerate(terms):
        out = jnp.where(field == f + 4, total(term), out)
    out = jnp.where(slot == (both & 7), out, 0.0)
    parts = jnp.concatenate(split3(out), axis=1)
    got = jnp.dot(jnp.concatenate(hits, axis=1), parts, preferred_element_type=jnp.float32)
    send[pl.ds(0, W, AHEAD), :] = got[:, :W] + got[:, W : 2 * W] + got[:, 2 * W :]


def soil_kernel(soil, coef, rain, after, owner, reach, soil_mid, mid0, share, hit, spot, water_v, coef_v, out_v, rain_v, sems, out_sems):
    del after
    layers = water_v.shape[0]
    loads = run_all([pltpu.make_async_copy(rain, rain_v, sems.at[0, layers])])
    for layer in range(layers):
        loads.append(pltpu.make_async_copy(soil.at[:, layer, :], water_v.at[layer], sems.at[0, layer]))
        loads.append(pltpu.make_async_copy(coef.at[:, layer, :], coef_v.at[layer], sems.at[1, layer]))
    run_all(loads[1:])
    sub = iota((W, W), 0)
    for step in range(owner.shape[0]):
        at = slice(step * CHUNK, (step + 1) * CHUNK)
        at_reach = jnp.broadcast_to(reach[step : step + 1, :], (W, CHUNK))
        hit[at, :] = jnp.transpose((at_reach == sub).astype(jnp.float32)).astype(jnp.bfloat16)
        place = jnp.broadcast_to(owner[step : step + 1, :].astype(jnp.float32), (W, CHUNK))
        spot[at, :] = jnp.transpose(place).astype(jnp.int32)
    loads[0].wait()
    stores = []
    coming = surface = None
    for layer in range(layers):
        wait_all(loads[1 + 2 * layer : 3 + 2 * layer])
        water = water_v[layer]
        if layer == 0:
            surface = rain_v[...] * water * water
            coming = rain_v[...] - surface
        drained = coef_v[layer] * water * water * water
        mid = water + coming - drained
        coming = drained
        if layer == 0:
            mid0[...] = mid
        else:
            out_v[layer] = mid
            copy = pltpu.make_async_copy(out_v.at[layer], soil_mid.at[:, layer, :], out_sems.at[layer])
            copy.start()
            stores.append(copy)
    share[...] = (surface + coming) * (1.0 / SUB)
    wait_all(stores)


def sort_columns(v):
    sub = iota((8, W), 0)
    size = 2
    while size <= W:
        j = size // 2
        while j >= 1:
            for a in range(16):
                if j >= 16:
                    d = j >> 4
                    clear = (sub & d) == 0
                    other = jnp.where(clear, pltpu.roll(v[a], 8 - d, 0), pltpu.roll(v[a], d, 0))
                    bit = sub // d & 1
                    lower = bit == (sub // (size >> 4) & 1) if size < W else clear
                    v[a] = jnp.where(lower, jnp.minimum(v[a], other), jnp.maximum(v[a], other))
                elif not a & j:
                    b = a | j
                    low, high = jnp.minimum(v[a], v[b]), jnp.maximum(v[a], v[b])
                    if size < 16:
                        v[a], v[b] = (high, low) if a & size else (low, high)
                    elif size == W:
                        v[a], v[b] = low, high
                    else:
                        up = (sub & (size >> 4)) == 0
                        v[a], v[b] = jnp.where(up, low, high), jnp.where(up, high, low)
            j //= 2
        size *= 2
    return v


def river_tables(recv, tables):
    lag = jnp.transpose(recv[pl.ds(1, W, AHEAD), :])
    volume = jnp.transpose(recv[pl.ds(2, W, AHEAD), :])
    row = iota((W, W), 0)
    weight = 1.0 / (1.0 + lag)
    product = prefix = suffix = weight
    by = 1
    k = 0
    while by < W:
        ok = row >= by
        tables[k] = jnp.where(ok, product, 0.0)
        product = product * pltpu.roll(product, by, 0)
        prefix = prefix * jnp.where(ok, pltpu.roll(prefix, by, 0), 1.0)
        suffix = suffix * jnp.where(row < W - by, pltpu.roll(suffix, W - by, 0), 1.0)
        by *= 2
        k += 1
    for i, value in enumerate((prefix, suffix, weight, lag, volume)):
        tables[k + i] = value
    whole = jnp.transpose(jnp.broadcast_to(prefix[W - 1 : W, :], (W, W)))
    factor = jnp.where(row < W - RIVERS, pltpu.roll(whole, W - RIVERS, 0), 0.0)
    reached = (iota((W, W), 1) == row + RIVERS).astype(jnp.float32)
    by = RIVERS
    while by < W:
        reached = reached + factor * pltpu.roll(reached, W - by, 0)
        factor = factor * pltpu.roll(factor, W - by, 0)
        by *= 2
    for i, part in enumerate(split3(reached)):
        tables[k + 5 + i] = part.astype(jnp.float32)


def inflow_kernel(
    share, hit, spot, storage, rate, links, recv, gains, tables, key_v, s_v, share_v, hit_v, spot_v, sems
):
    pairs = ((share, share_v), (hit, hit_v), (spot, spot_v))
    loads = run_all([pltpu.make_async_copy(src, dst, sems.at[k]) for k, (src, dst) in enumerate(pairs)])
    shape = storage.shape
    sub = iota((8, W), 0)
    for step in range(shape[0] // CHUNK):
        at = slice(step * CHUNK, (step + 1) * CHUNK)
        turned = jnp.transpose(links[at, :].astype(jnp.float32))
        tiles = [
            turned[8 * a : 8 * a + 8, :] * float(W) + (sub + 8 * a).astype(jnp.float32)
            for a in range(W // 8)
        ]
        key_v[at, :] = jnp.transpose(jnp.concatenate(sort_columns(tiles), axis=0))
    river_tables(recv, tables)

    lane = iota(shape, 1)
    key = key_v[...].astype(jnp.int32)
    order = key & (W - 1)
    dest = key >> 7
    count = jnp.zeros(shape, jnp.int32)
    for shift in (64, 32, 16, 8, 4, 2, 1):
        last = count + (shift - 1)
        found = gat(dest, ((last & 15) << 3) | (last >> 4))
        count = jnp.where(found <= lane, count + shift, count)
    earlier = jnp.where(lane == 0, 0, pltpu.roll(count, 1, 1))
    q = iota((W, W), 0)
    ahead = ((q >> 3) + 16 * (q & 7) < iota((W, W), 1)).astype(jnp.bfloat16)
    ahead = jnp.concatenate([ahead] * 3, axis=0)
    s_v[...] = storage[...]
    wait_all(loads)
    for n in range(SUB):
        s = s_v[...]
        release = rate[...] * s
        parts = jnp.concatenate(split3(gat(release, order)), axis=1)
        run = jnp.dot(parts, ahead, preferred_element_type=jnp.float32)
        gain = share_v[...] + (gat(run, count) - gat(run, earlier))
        if n == 0:
            parts = jnp.concatenate(split3(1.0 / (1.0 + tables[11])), axis=1)
            seen = jnp.dot(hit_v[...], parts, preferred_element_type=jnp.float32)
            back = gat(seen[:, :W] + seen[:, W : 2 * W] + seen[:, 2 * W :], spot_v[...])
            gains[n] = s - release * jnp.where(links[...] == W, back, 1.0) + gain
        else:
            gains[n] = gain
        s_v[...] = s + gain - release


def reach_kernel(recv, volume, out):
    got = recv[pl.ds(0, W, AHEAD), :]
    turned = jnp.transpose(got)
    lane = iota((W, W), 1)
    total = jnp.zeros((48, W), jnp.float32)
    for c in range(8):
        at = jnp.broadcast_to(got[:, c * 16 + 10 : c * 16 + 11], (W, W)).astype(jnp.int32)
        hit = (at == lane).astype(jnp.bfloat16)
        parts = jnp.concatenate(split3(turned[c * 16 : c * 16 + 16, :]), axis=0)
        total += jnp.dot(parts, hit, preferred_element_type=jnp.float32)
    total = total[:16, :] + total[16:32, :] + total[32:, :]
    row = lambda f: total[f : f + 1, :]
    vol = volume[...]
    back = 1.0 / (1.0 + vol)
    lateral = back * row(0) * (1.0 / W)
    s1 = row(0) - back * row(1) + row(4)
    s2 = row(1) - back * row(2) + row(5)
    s3 = row(2) - back * row(3) + row(6)
    fields = (lateral, s1, s2, s3, row(7), row(8), row(9))
    wide = [jnp.broadcast_to(value, (8, W)) for value in fields]
    sub = iota((8, W), 0)
    period = []
    for k in range(FIELDS):
        tile = jnp.zeros((8, W), jnp.float32)
        for i in range(8):
            tile = jnp.where(sub == i, wide[(k * 8 + i) % FIELDS], tile)
        period.append(tile)
    for k in range(W // 8):
        for f in range(FIELDS):
            at = (k * FIELDS + f) * 8
            out[at : at + 8, :] = period[f]


def finish_kernel(
    fields, tables, gains, rate, links, hit, spot, mid0, soil_mid, soil_out, storage_out, section,
    table, flow_ref, hit_v, spot_v, mid_v, out_v, top_v, section_v, sems, out_sems, section_sem
):
    del soil_mid
    loads = run_all(
        [
            pltpu.make_async_copy(src, dst, sems.at[k])
            for k, (src, dst) in enumerate(
                (
                    (hit, hit_v),
                    (spot, spot_v),
                    (mid0, mid_v),
                )
            )
        ]
    )
    field = lambda f: jnp.transpose(fields[pl.ds(f, W, FIELDS), :])
    levels = 7
    prefix, suffix, weight, lag, volume = (tables[levels + k] for k in range(5))
    crossing = jnp.concatenate([tables[levels + 5 + k].astype(jnp.bfloat16) for k in range(3)], axis=1)
    lateral = field(0)
    s1, s2, s3 = field(1), field(2), field(3)
    c11, c12, c21 = field(4), field(5), field(6)
    flow = volume
    for n in range(SUB):
        if n:
            back = 1.0 / (1.0 + volume)
            for part, value in enumerate(split3(back)):
                at = (part * (SUB - 1) + n - 1) * W
                table[:, at : at + W] = value
        if n == 1:
            lateral = back * s1 * (1.0 / W)
            s1, s2 = s1 - back * s2 + c11, s2 - back * s3 + c12
        elif n == 2:
            lateral = back * s1 * (1.0 / W)
            s1 = s1 - back * s2 + c21
        elif n == 3:
            lateral = back * s1 * (1.0 / W)
        entering = volume + lateral
        ends = jnp.sum(entering * suffix, axis=0, keepdims=True)
        ends = jnp.concatenate([jnp.broadcast_to(part, (16, W)) for part in split3(ends)], axis=0)
        head = jnp.dot(ends, crossing, preferred_element_type=jnp.float32)
        head = head[:8, :] + head[16:24, :] + head[32:40, :]
        head = head[:1, :W] + head[:1, W : 2 * W] + head[:1, 2 * W :]
        run = weight * entering
        for k in range(levels):
            run = run + tables[k] * pltpu.roll(run, 1 << k, 0)
        flow = run + prefix * head
        volume = lag * flow
    flow_ref[...] = flow

    wait_all(loads)
    stores = []
    blocks = out_v.shape[0]
    for step in range(blocks // CHUNK):
        at = slice(step * CHUNK, (step + 1) * CHUNK)
        got = jnp.dot(hit_v[at, :], table[...], preferred_element_type=jnp.float32)
        place = spot_v[at, :]
        s, r = gains[0, at, :], rate[at, :]
        leaves = links[at, :] == W
        for n in range(1, SUB):
            part = lambda k: got[:, (k * (SUB - 1) + n - 1) * W : (k * (SUB - 1) + n) * W]
            back = gat(part(0) + part(1) + part(2), place)
            s = s - r * jnp.where(leaves, back, 1.0) * s + gains[n, at, :]
        out_v[at, :] = s
        top = mid_v[at, :]
        top_v[at, :] = top + recharge_share * (s / (s + 1.0)) * (1.0 - top)
        where = pl.ds(step * CHUNK, CHUNK)
        stores += run_all(
            [
                pltpu.make_async_copy(out_v.at[where], storage_out.at[where], out_sems.at[0, step]),
                pltpu.make_async_copy(top_v.at[where], soil_out.at[where, 0, :], out_sems.at[1, step]),
            ]
        )
        if step == 1:
            flow_ref[...] = jnp.transpose(flow_ref[...])
            section_v[...] = jnp.log1p(flow_ref[pl.ds(lax.axis_index(("tile", "grp")), 1), :])
            stores += run_all([pltpu.make_async_copy(section_v, section, section_sem)])
    wait_all(stores)


def local(
    soil_water,
    rainfall,
    drain_coef,
    cell_storage,
    release_rate,
    downstream,
    block_owner,
    outlet_reach,
    river_storage,
    river_lag,
):
    axes = ("tile", "grp")
    blocks = block_owner.shape[0]
    steps = blocks // CHUNK
    layers = soil_water.shape[0]

    def tiles(x):
        return x.reshape(layers, blocks, W).transpose(1, 0, 2)

    soil, coef = tiles(soil_water), tiles(drain_coef)
    rain, storage, rate, links = (
        x.reshape(blocks, W) for x in (rainfall, cell_storage, release_rate, downstream)
    )
    owner = block_owner.reshape(steps, CHUNK)
    reach = outlet_reach.reshape(steps, CHUNK)

    f32 = jnp.float32
    i32 = jnp.int32
    b16 = jnp.bfloat16
    shaped = jax.ShapeDtypeStruct
    vmem = pl.BlockSpec(memory_space=pltpu.VMEM)
    hbm = pl.BlockSpec(memory_space=pltpu.HBM)
    params = pltpu.CompilerParams(vmem_limit_bytes=24 * MB)
    scratch = lambda dtype, *shape: pltpu.VMEM(shape, dtype)
    flat = lambda dtype: scratch(dtype, blocks, W)
    stay = lambda x: pltpu.with_memory_space_constraint(x, pltpu.HBM)
    sems = lambda *shape: pltpu.SemaphoreType.DMA(shape)
    cost = lambda flops, moved: pl.CostEstimate(flops=flops, bytes_accessed=moved, transcendentals=0)

    send = pl.pallas_call(
        moments_kernel,
        in_specs=[hbm] * 10,
        out_specs=vmem,
        out_shape=shaped((W * AHEAD, W), f32),
        scratch_shapes=[flat(f32)] * 6
        + [flat(i32), flat(f32)]
        + [scratch(i32, steps, CHUNK)] * 2
        + [scratch(f32, 1, W)] * 2
        + [sems(11)],
        compiler_params=params,
        name="moments",
    )(*map(stay, (soil, coef, rain, storage, rate, links, owner, reach, river_storage, river_lag)))

    def exchange(rows, count):
        rows = rows.reshape(W, 1, count * W)
        rows = lax.all_to_all(rows, axes, split_axis=0, concat_axis=0, tiled=True)
        return rows.reshape(W * count, W)

    recv = exchange(send, AHEAD)

    soil_mid, mid0, share, hit, spot = pl.pallas_call(
        soil_kernel,
        in_specs=[hbm] * 4 + [vmem] * 2,
        out_specs=[hbm] + [vmem] * 4,
        out_shape=[
            pltpu.HBM((blocks, layers, W), f32),
            pltpu.HBM((blocks, W), f32),
            pltpu.HBM((blocks, W), f32),
            pltpu.HBM((blocks, W), b16),
            pltpu.HBM((blocks, W), i32),
        ],
        scratch_shapes=[scratch(f32, layers, blocks, W)] * 3 + [flat(f32), sems(2, layers + 1), sems(layers)],
        compiler_params=params,
        cost_estimate=cost(3_000_000, 10 * MB),
        name="soil",
    )(*map(stay, (soil, coef, rain, send, owner, reach)))

    recv, spot = lax.optimization_barrier((recv, spot))

    fields = pl.pallas_call(
        reach_kernel,
        in_specs=[vmem] * 2,
        out_specs=vmem,
        out_shape=shaped((W * FIELDS, W), f32),
        compiler_params=params,
        name="reaches",
    )(recv, river_storage)
    fields, recv = lax.optimization_barrier((fields, recv))
    fields = exchange(fields, FIELDS)

    gains, tables = pl.pallas_call(
        inflow_kernel,
        in_specs=[hbm] * 3 + [vmem] * 4,
        out_specs=[vmem] * 2,
        out_shape=[shaped((SUB, blocks, W), f32), shaped((15, W, W), f32)],
        scratch_shapes=[flat(f32)] * 3 + [flat(b16), flat(i32), sems(3)],
        compiler_params=params,
        cost_estimate=cost(10_000_000, 16 * MB),
        name="inflow",
    )(*map(stay, (share, hit, spot)), storage, rate, links, recv)

    soil_out, storage_out, section = pl.pallas_call(
        finish_kernel,
        in_specs=[vmem] * 5 + [hbm] * 4,
        out_specs=[hbm] * 3,
        out_shape=[
            shaped((blocks, layers, W), f32),
            shaped((blocks, W), f32),
            shaped((1, W), f32),
        ],
        scratch_shapes=[
            scratch(b16, W, 3 * (SUB - 1) * W),
            scratch(f32, W, W),
            flat(b16),
            flat(i32),
            flat(f32),
            flat(f32),
            flat(f32),
            scratch(f32, 1, W),
            sems(3),
            sems(2, steps),
            pltpu.SemaphoreType.DMA,
        ],
        input_output_aliases={8: 0},
        compiler_params=params,
        name="finish",
    )(fields, tables, gains, rate, links, *map(stay, (hit, spot, mid0, soil_mid)))

    soil_out = soil_out.transpose(1, 0, 2).reshape(layers, blocks * W)
    return (soil_out, storage_out.reshape(-1), section)


def solution(mesh):
    placed = (
        P(None, ("tile", "grp")),
        P(("tile", "grp")),
        P(None, ("tile", "grp")),
        P(("tile", "grp")),
        P(("tile", "grp")),
        P(("tile", "grp")),
        P(("tile", "grp"), None),
        P(("tile", "grp")),
        P("grp", "tile"),
        P("grp", "tile"),
    )
    return jax.shard_map(
        local,
        mesh=mesh,
        in_specs=placed,
        out_specs=(P(None, ("tile", "grp")), P(("tile", "grp")), P("grp", "tile")),
        check_vma=False,
    )
```

```python
import jax
import jax.numpy as jnp
from jax import lax
from jax.experimental import pallas as pl
from jax.experimental.pallas import tpu as pltpu
from jax.sharding import PartitionSpec as P

SUB = 4
RIVERS = 4
recharge_share = 0.2

W = 128
CHUNK = 128
AHEAD = 3
FIELDS = 7
MB = 1024 * 1024


def gat(values, index):
    return jnp.take_along_axis(values, index, axis=1, mode="promise_in_bounds")


def iota(shape, dim):
    return lax.broadcasted_iota(jnp.int32, shape, dim)


def split3(x):
    hi = x.astype(jnp.bfloat16)
    rest = x - hi.astype(jnp.float32)
    mid = rest.astype(jnp.bfloat16)
    low = (rest - mid.astype(jnp.float32)).astype(jnp.bfloat16)
    return hi, mid, low


def run_all(copies):
    for copy in copies:
        copy.start()
    return copies


def wait_all(copies):
    for copy in copies:
        copy.wait()


def moments_kernel(
    soil, coef, rain, storage, rate, links, owner_hbm, reach_hbm, volume_hbm, lag_hbm, send,
    top, low, low_coef, rain_v, s_v, r_v, to_v, pack_v, owner, reach, volume, lag, sems
):
    lane = iota((W, W), 1)
    sub = iota((W, W), 0)
    pairs = (
        (owner_hbm, owner),
        (reach_hbm, reach),
        (volume_hbm, volume),
        (lag_hbm, lag),
        (links, to_v),
        (rate, r_v),
        (storage, s_v),
        (soil.at[:, 0, :], top),
        (soil.at[:, 5, :], low),
        (coef.at[:, 5, :], low_coef),
        (rain, rain_v),
    )
    loads = run_all([pltpu.make_async_copy(src, dst, sems.at[k]) for k, (src, dst) in enumerate(pairs)])

    small, loads = loads[:4], loads[4:]
    wait_all(small)
    before = (sub < lane).astype(jnp.bfloat16)
    hits = []
    carry = jnp.zeros((W, 1), jnp.float32)
    for step in range(owner.shape[0]):
        own = jnp.broadcast_to(owner[step : step + 1, :], (W, CHUNK))
        hit = (own == sub).astype(jnp.float32)
        hit16 = hit.astype(jnp.bfloat16)
        hits.append(hit16)
        seen = jnp.dot(hit16, before, preferred_element_type=jnp.float32) + carry
        carry = carry + jnp.sum(hit, axis=1, keepdims=True)
        rank = jnp.sum(hit * seen, axis=0, keepdims=True)
        both = rank + 8.0 * reach[step : step + 1, :].astype(jnp.float32)
        both = jnp.transpose(jnp.broadcast_to(both, (W, CHUNK)))
        pack_v[step * CHUNK : (step + 1) * CHUNK, :] = both
    send[pl.ds(1, W, AHEAD), :] = jnp.broadcast_to(lag[...], (W, W))
    send[pl.ds(2, W, AHEAD), :] = jnp.broadcast_to(volume[...], (W, W))

    field = iota(s_v.shape, 1) & 15
    slot = iota(s_v.shape, 1) >> 4
    both = pack_v[...].astype(jnp.int32)
    out = (both >> 3).astype(jnp.float32)
    total = lambda term: jnp.sum(term, axis=1, keepdims=True)

    wait_all(loads[:2])
    r, down = r_v[...], to_v[...]
    leaves = down == W
    to = down & (W - 1)
    follow = lambda v: jnp.where(leaves, 0.0, gat(v, to))
    a1 = jnp.where(leaves, r, 0.0)
    a2 = a1 * r
    a3 = a2 * r
    g = follow(a1)
    w_1 = r * g
    w_2 = w_1 * g
    w_3 = w_2 * g
    x_1 = r * follow(w_1)
    x_2 = r * follow(w_2)
    z = w_1 * (1.0 - r) + x_1
    y = r * follow(z)
    loads[2].wait()
    s = s_v[...]
    for f, a in enumerate((a1, a2, a3, a3 * r)):
        out = jnp.where(field == f, total(a * s), out)
    wait_all(loads[3:])
    w0, w5 = top[...], low[...]
    share = (rain_v[...] * w0 * w0 + low_coef[...] * w5 * w5 * w5) * (1.0 / SUB)
    e1 = (1.0 - r) * s + share
    h1 = a1 * share
    h2 = a2 * share
    terms = (
        h1 + w_1 * s,
        h2 + w_2 * s,
        a3 * share + w_3 * s,
        h1 + w_1 * e1 + x_1 * s,
        h2 + w_2 * e1 + x_2 * s,
        h1 + w_1 * share + z * e1 + y * s,
    )
    for f, term in enumerate(terms):
        out = jnp.where(field == f + 4, total(term), out)
    out = jnp.where(slot == (both & 7), out, 0.0)
    parts = jnp.concatenate(split3(out), axis=1)
    got = jnp.dot(jnp.concatenate(hits, axis=1), parts, preferred_element_type=jnp.float32)
    send[pl.ds(0, W, AHEAD), :] = got[:, :W] + got[:, W : 2 * W] + got[:, 2 * W :]


def soil_kernel(
    soil, coef, rain, after, owner_hbm, reach_hbm, soil_mid, mid0, share, hit, spot,
    water_v, coef_v, out_v, rain_v, owner, reach, sems, out_sems, small_sems
):
    del after
    small = run_all(
        [
            pltpu.make_async_copy(owner_hbm, owner, small_sems.at[0]),
            pltpu.make_async_copy(reach_hbm, reach, small_sems.at[1]),
        ]
    )
    layers = water_v.shape[0]
    loads = run_all([pltpu.make_async_copy(rain, rain_v, sems.at[0, layers])])
    for layer in range(layers):
        loads.append(pltpu.make_async_copy(soil.at[:, layer, :], water_v.at[layer], sems.at[0, layer]))
        loads.append(pltpu.make_async_copy(coef.at[:, layer, :], coef_v.at[layer], sems.at[1, layer]))
    run_all(loads[1:])
    wait_all(small)
    sub = iota((W, W), 0)
    for step in range(owner.shape[0]):
        at = slice(step * CHUNK, (step + 1) * CHUNK)
        at_reach = jnp.broadcast_to(reach[step : step + 1, :], (W, CHUNK))
        hit[at, :] = jnp.transpose((at_reach == sub).astype(jnp.float32)).astype(jnp.bfloat16)
        place = jnp.broadcast_to(owner[step : step + 1, :].astype(jnp.float32), (W, CHUNK))
        spot[at, :] = jnp.transpose(place).astype(jnp.int32)
    loads[0].wait()
    stores = []
    coming = surface = None
    for layer in range(layers):
        wait_all(loads[1 + 2 * layer : 3 + 2 * layer])
        water = water_v[layer]
        if layer == 0:
            surface = rain_v[...] * water * water
            coming = rain_v[...] - surface
        drained = coef_v[layer] * water * water * water
        mid = water + coming - drained
        coming = drained
        if layer == 0:
            mid0[...] = mid
        else:
            out_v[layer] = mid
            copy = pltpu.make_async_copy(out_v.at[layer], soil_mid.at[:, layer, :], out_sems.at[layer])
            copy.start()
            stores.append(copy)
    share[...] = (surface + coming) * (1.0 / SUB)
    wait_all(stores)


def sort_columns(v):
    sub = iota((8, W), 0)
    size = 2
    while size <= W:
        j = size // 2
        while j >= 1:
            for a in range(16):
                if j >= 16:
                    d = j >> 4
                    clear = (sub & d) == 0
                    other = jnp.where(clear, pltpu.roll(v[a], 8 - d, 0), pltpu.roll(v[a], d, 0))
                    bit = sub // d & 1
                    lower = bit == (sub // (size >> 4) & 1) if size < W else clear
                    v[a] = jnp.where(lower, jnp.minimum(v[a], other), jnp.maximum(v[a], other))
                elif not a & j:
                    b = a | j
                    low, high = jnp.minimum(v[a], v[b]), jnp.maximum(v[a], v[b])
                    if size < 16:
                        v[a], v[b] = (high, low) if a & size else (low, high)
                    elif size == W:
                        v[a], v[b] = low, high
                    else:
                        up = (sub & (size >> 4)) == 0
                        v[a], v[b] = jnp.where(up, low, high), jnp.where(up, high, low)
            j //= 2
        size *= 2
    return v


def river_tables(recv, tables):
    lag = jnp.transpose(recv[pl.ds(1, W, AHEAD), :])
    volume = jnp.transpose(recv[pl.ds(2, W, AHEAD), :])
    row = iota((W, W), 0)
    weight = 1.0 / (1.0 + lag)
    product = prefix = suffix = weight
    by = 1
    k = 0
    while by < W:
        ok = row >= by
        tables[k] = jnp.where(ok, product, 0.0)
        product = product * pltpu.roll(product, by, 0)
        prefix = prefix * jnp.where(ok, pltpu.roll(prefix, by, 0), 1.0)
        suffix = suffix * jnp.where(row < W - by, pltpu.roll(suffix, W - by, 0), 1.0)
        by *= 2
        k += 1
    for i, value in enumerate((prefix, suffix, weight, lag, volume)):
        tables[k + i] = value
    whole = jnp.transpose(jnp.broadcast_to(prefix[W - 1 : W, :], (W, W)))
    factor = jnp.where(row < W - RIVERS, pltpu.roll(whole, W - RIVERS, 0), 0.0)
    reached = (iota((W, W), 1) == row + RIVERS).astype(jnp.float32)
    by = RIVERS
    while by < W:
        reached = reached + factor * pltpu.roll(reached, W - by, 0)
        factor = factor * pltpu.roll(factor, W - by, 0)
        by *= 2
    for i, part in enumerate(split3(reached)):
        tables[k + 5 + i] = part.astype(jnp.float32)


def inflow_kernel(
    share, hit, spot, storage, rate, links, recv, gains, tables, key_v, s_v, share_v, hit_v, spot_v, sems
):
    pairs = ((share, share_v), (hit, hit_v), (spot, spot_v))
    loads = run_all([pltpu.make_async_copy(src, dst, sems.at[k]) for k, (src, dst) in enumerate(pairs)])
    shape = storage.shape
    sub = iota((8, W), 0)
    for step in range(shape[0] // CHUNK):
        at = slice(step * CHUNK, (step + 1) * CHUNK)
        turned = jnp.transpose(links[at, :].astype(jnp.float32))
        tiles = [
            turned[8 * a : 8 * a + 8, :] * float(W) + (sub + 8 * a).astype(jnp.float32)
            for a in range(W // 8)
        ]
        key_v[at, :] = jnp.transpose(jnp.concatenate(sort_columns(tiles), axis=0))
    river_tables(recv, tables)

    lane = iota(shape, 1)
    key = key_v[...].astype(jnp.int32)
    order = key & (W - 1)
    dest = key >> 7
    count = jnp.zeros(shape, jnp.int32)
    for shift in (64, 32, 16, 8, 4, 2, 1):
        last = count + (shift - 1)
        found = gat(dest, ((last & 15) << 3) | (last >> 4))
        count = jnp.where(found <= lane, count + shift, count)
    earlier = jnp.where(lane == 0, 0, pltpu.roll(count, 1, 1))
    q = iota((W, W), 0)
    ahead = ((q >> 3) + 16 * (q & 7) < iota((W, W), 1)).astype(jnp.bfloat16)
    ahead = jnp.concatenate([ahead] * 3, axis=0)
    s_v[...] = storage[...]
    wait_all(loads)
    for n in range(SUB):
        s = s_v[...]
        release = rate[...] * s
        parts = jnp.concatenate(split3(gat(release, order)), axis=1)
        run = jnp.dot(parts, ahead, preferred_element_type=jnp.float32)
        gain = share_v[...] + (gat(run, count) - gat(run, earlier))
        if n == 0:
            parts = jnp.concatenate(split3(1.0 / (1.0 + tables[11])), axis=1)
            seen = jnp.dot(hit_v[...], parts, preferred_element_type=jnp.float32)
            back = gat(seen[:, :W] + seen[:, W : 2 * W] + seen[:, 2 * W :], spot_v[...])
            gains[n] = s - release * jnp.where(links[...] == W, back, 1.0) + gain
        else:
            gains[n] = gain
        s_v[...] = s + gain - release


def reach_kernel(recv, volume, out):
    got = recv[pl.ds(0, W, AHEAD), :]
    turned = jnp.transpose(got)
    lane = iota((W, W), 1)
    hits, parts = [], []
    for c in range(8):
        at = jnp.broadcast_to(got[:, c * 16 + 10 : c * 16 + 11], (W, W)).astype(jnp.int32)
        hits.append((at == lane).astype(jnp.bfloat16))
        parts.append(jnp.concatenate(split3(turned[c * 16 : c * 16 + 16, :]), axis=0))
    total = jnp.dot(
        jnp.concatenate(parts, axis=1), jnp.concatenate(hits, axis=0), preferred_element_type=jnp.float32
    )
    total = total[:16, :] + total[16:32, :] + total[32:, :]
    row = lambda f: total[f : f + 1, :]
    vol = volume[...]
    back = 1.0 / (1.0 + vol)
    lateral = back * row(0) * (1.0 / W)
    s1 = row(0) - back * row(1) + row(4)
    s2 = row(1) - back * row(2) + row(5)
    s3 = row(2) - back * row(3) + row(6)
    fields = (lateral, s1, s2, s3, row(7), row(8), row(9))
    wide = [jnp.broadcast_to(value, (8, W)) for value in fields]
    sub = iota((8, W), 0)
    period = []
    for k in range(FIELDS):
        tile = jnp.zeros((8, W), jnp.float32)
        for i in range(8):
            tile = jnp.where(sub == i, wide[(k * 8 + i) % FIELDS], tile)
        period.append(tile)
    for k in range(W // 8):
        for f in range(FIELDS):
            at = (k * FIELDS + f) * 8
            out[at : at + 8, :] = period[f]


def finish_kernel(
    fields, tables, gains, rate, links, hit, spot, mid0, soil_mid, soil_out, storage_out, section,
    table, flow_ref, hit_v, spot_v, mid_v, out_v, top_v, section_v, sems, out_sems, section_sem
):
    del soil_mid
    loads = run_all(
        [
            pltpu.make_async_copy(src, dst, sems.at[k])
            for k, (src, dst) in enumerate(
                (
                    (hit, hit_v),
                    (spot, spot_v),
                    (mid0, mid_v),
                )
            )
        ]
    )
    field = lambda f: jnp.transpose(fields[pl.ds(f, W, FIELDS), :])
    levels = 7
    prefix, suffix, weight, lag, volume = (tables[levels + k] for k in range(5))
    crossing = jnp.concatenate([tables[levels + 5 + k].astype(jnp.bfloat16) for k in range(3)], axis=1)
    lateral = field(0)
    s1, s2, s3 = field(1), field(2), field(3)
    c11, c12, c21 = field(4), field(5), field(6)
    flow = volume
    for n in range(SUB):
        if n:
            back = 1.0 / (1.0 + volume)
            for part, value in enumerate(split3(back)):
                at = (part * (SUB - 1) + n - 1) * W
                table[:, at : at + W] = value
        if n == 1:
            lateral = back * s1 * (1.0 / W)
            s1, s2 = s1 - back * s2 + c11, s2 - back * s3 + c12
        elif n == 2:
            lateral = back * s1 * (1.0 / W)
            s1 = s1 - back * s2 + c21
        elif n == 3:
            lateral = back * s1 * (1.0 / W)
        entering = volume + lateral
        ends = jnp.sum(entering * suffix, axis=0, keepdims=True)
        ends = jnp.concatenate([jnp.broadcast_to(part, (16, W)) for part in split3(ends)], axis=0)
        head = jnp.dot(ends, crossing, preferred_element_type=jnp.float32)
        head = head[:8, :] + head[16:24, :] + head[32:40, :]
        head = head[:1, :W] + head[:1, W : 2 * W] + head[:1, 2 * W :]
        run = weight * entering
        for k in range(levels):
            run = run + tables[k] * pltpu.roll(run, 1 << k, 0)
        flow = run + prefix * head
        volume = lag * flow
    flow_ref[...] = flow

    wait_all(loads)
    stores = []
    blocks = out_v.shape[0]
    for step in range(blocks // CHUNK):
        at = slice(step * CHUNK, (step + 1) * CHUNK)
        got = jnp.dot(hit_v[at, :], table[...], preferred_element_type=jnp.float32)
        place = spot_v[at, :]
        s, r = gains[0, at, :], rate[at, :]
        leaves = links[at, :] == W
        for n in range(1, SUB):
            part = lambda k: got[:, (k * (SUB - 1) + n - 1) * W : (k * (SUB - 1) + n) * W]
            back = gat(part(0) + part(1) + part(2), place)
            s = s - r * jnp.where(leaves, back, 1.0) * s + gains[n, at, :]
        out_v[at, :] = s
        top = mid_v[at, :]
        top_v[at, :] = top + recharge_share * (s / (s + 1.0)) * (1.0 - top)
        where = pl.ds(step * CHUNK, CHUNK)
        stores += run_all(
            [
                pltpu.make_async_copy(out_v.at[where], storage_out.at[where], out_sems.at[0, step]),
                pltpu.make_async_copy(top_v.at[where], soil_out.at[where, 0, :], out_sems.at[1, step]),
            ]
        )
        if step == 1:
            flow_ref[...] = jnp.transpose(flow_ref[...])
            section_v[...] = jnp.log1p(flow_ref[pl.ds(lax.axis_index(("tile", "grp")), 1), :])
            stores += run_all([pltpu.make_async_copy(section_v, section, section_sem)])
    wait_all(stores)


def local(
    soil_water,
    rainfall,
    drain_coef,
    cell_storage,
    release_rate,
    downstream,
    block_owner,
    outlet_reach,
    river_storage,
    river_lag,
):
    axes = ("tile", "grp")
    blocks = block_owner.shape[0]
    steps = blocks // CHUNK
    layers = soil_water.shape[0]

    def tiles(x):
        return x.reshape(layers, blocks, W).transpose(1, 0, 2)

    soil, coef = tiles(soil_water), tiles(drain_coef)
    rain, storage, rate, links = (
        x.reshape(blocks, W) for x in (rainfall, cell_storage, release_rate, downstream)
    )
    owner = block_owner.reshape(steps, CHUNK)
    reach = outlet_reach.reshape(steps, CHUNK)

    f32 = jnp.float32
    i32 = jnp.int32
    b16 = jnp.bfloat16
    shaped = jax.ShapeDtypeStruct
    vmem = pl.BlockSpec(memory_space=pltpu.VMEM)
    hbm = pl.BlockSpec(memory_space=pltpu.HBM)
    params = pltpu.CompilerParams(vmem_limit_bytes=24 * MB)
    scratch = lambda dtype, *shape: pltpu.VMEM(shape, dtype)
    flat = lambda dtype: scratch(dtype, blocks, W)
    stay = lambda x: pltpu.with_memory_space_constraint(x, pltpu.HBM)
    sems = lambda *shape: pltpu.SemaphoreType.DMA(shape)
    cost = lambda flops, moved: pl.CostEstimate(flops=flops, bytes_accessed=moved, transcendentals=0)

    send = pl.pallas_call(
        moments_kernel,
        in_specs=[hbm] * 10,
        out_specs=vmem,
        out_shape=shaped((W * AHEAD, W), f32),
        scratch_shapes=[flat(f32)] * 6
        + [flat(i32), flat(f32)]
        + [scratch(i32, steps, CHUNK)] * 2
        + [scratch(f32, 1, W)] * 2
        + [sems(11)],
        compiler_params=params,
        name="moments",
    )(*map(stay, (soil, coef, rain, storage, rate, links, owner, reach, river_storage, river_lag)))

    def exchange(rows, count):
        rows = rows.reshape(W, 1, count * W)
        rows = lax.all_to_all(rows, axes, split_axis=0, concat_axis=0, tiled=True)
        return rows.reshape(W * count, W)

    recv = exchange(send, AHEAD)

    soil_mid, mid0, share, hit, spot = pl.pallas_call(
        soil_kernel,
        in_specs=[hbm] * 6,
        out_specs=[hbm] + [vmem] * 4,
        out_shape=[
            pltpu.HBM((blocks, layers, W), f32),
            pltpu.HBM((blocks, W), f32),
            pltpu.HBM((blocks, W), f32),
            pltpu.HBM((blocks, W), b16),
            pltpu.HBM((blocks, W), i32),
        ],
        scratch_shapes=[scratch(f32, layers, blocks, W)] * 3
        + [flat(f32)]
        + [scratch(i32, steps, CHUNK)] * 2
        + [sems(2, layers + 1), sems(layers), sems(2)],
        compiler_params=params,
        cost_estimate=cost(3_000_000, 10 * MB),
        name="soil",
    )(*map(stay, (soil, coef, rain, send, owner, reach)))

    recv, spot = lax.optimization_barrier((recv, spot))

    fields = pl.pallas_call(
        reach_kernel,
        in_specs=[vmem] * 2,
        out_specs=vmem,
        out_shape=shaped((W * FIELDS, W), f32),
        compiler_params=params,
        name="reaches",
    )(recv, river_storage)
    fields, recv = lax.optimization_barrier((fields, recv))
    fields = exchange(fields, FIELDS)

    gains, tables = pl.pallas_call(
        inflow_kernel,
        in_specs=[hbm] * 3 + [vmem] * 4,
        out_specs=[vmem] * 2,
        out_shape=[shaped((SUB, blocks, W), f32), shaped((15, W, W), f32)],
        scratch_shapes=[flat(f32)] * 3 + [flat(b16), flat(i32), sems(3)],
        compiler_params=params,
        cost_estimate=cost(10_000_000, 16 * MB),
        name="inflow",
    )(*map(stay, (share, hit, spot)), storage, rate, links, recv)

    soil_out, storage_out, section = pl.pallas_call(
        finish_kernel,
        in_specs=[vmem] * 5 + [hbm] * 4,
        out_specs=[hbm] * 3,
        out_shape=[
            shaped((blocks, layers, W), f32),
            shaped((blocks, W), f32),
            shaped((1, W), f32),
        ],
        scratch_shapes=[
            scratch(b16, W, 3 * (SUB - 1) * W),
            scratch(f32, W, W),
            flat(b16),
            flat(i32),
            flat(f32),
            flat(f32),
            flat(f32),
            scratch(f32, 1, W),
            sems(3),
            sems(2, steps),
            pltpu.SemaphoreType.DMA,
        ],
        input_output_aliases={8: 0},
        compiler_params=params,
        name="finish",
    )(fields, tables, gains, rate, links, *map(stay, (hit, spot, mid0, soil_mid)))

    soil_out = soil_out.transpose(1, 0, 2).reshape(layers, blocks * W)
    return (soil_out, storage_out.reshape(-1), section)


def solution(mesh):
    placed = (
        P(None, ("tile", "grp")),
        P(("tile", "grp")),
        P(None, ("tile", "grp")),
        P(("tile", "grp")),
        P(("tile", "grp")),
        P(("tile", "grp")),
        P(("tile", "grp"), None),
        P(("tile", "grp")),
        P("grp", "tile"),
        P("grp", "tile"),
    )
    return jax.shard_map(
        local,
        mesh=mesh,
        in_specs=placed,
        out_specs=(P(None, ("tile", "grp")), P(("tile", "grp")), P("grp", "tile")),
        check_vma=False,
    )
```
